32 devices in a mesh: dom: 8 (over z, y), hub: 4 (over x, core).
Axes of the slice: x: 2, y: 2, z: 4, core: 2. Of those that a mesh axis runs over, the one named last changes fastest.
Arguments:
- node_feats: bfloat16 [8, 4, 2048, 256], P('dom', 'hub'), may hold values from -6 to 6
- hub_feats: bfloat16 [1024, 256], P('hub'), may hold values from -6 to 6
- w_self: bfloat16 [256, 256], replicated, may hold values from -0.375 to 0.375
- w_neigh: bfloat16 [256, 256], replicated, may hold values from -0.375 to 0.375
- out_bias: float32 [256], replicated, may hold values from -3 to 3
- send_rows: int32 [8, 4, 8, 32], P('dom', 'hub'), may hold values from 0 to 2047, as said below
- send_counts: int32 [8, 4, 8], P('dom', 'hub'), may hold values from 0 to 32, as said below
- local_ids: int32 [8, 4, 16, 3], P('dom', 'hub'), may hold values from 0 to 15
- local_tiles: bfloat16 [8, 4, 16, 3, 128, 128], P('dom', 'hub'), may hold values from -0.5 to 0.5
- halo_ids: int32 [8, 4, 16, 2], P('dom', 'hub'), may hold values from 0 to 1
- halo_tiles: bfloat16 [8, 4, 16, 2, 128, 128], P('dom', 'hub'), may hold values from -0.5 to 0.5
- hub_ids: int32 [8, 4, 16, 2], P('dom', 'hub'), may hold values from 0 to 7
- hub_tiles: bfloat16 [8, 4, 16, 2, 128, 128], P('dom', 'hub'), may hold values from -0.5 to 0.5
- degree: int32 [8, 4, 2048], P('dom', 'hub'), may hold values from 1 to 8
- out_grad: bfloat16 [8, 4, 2048, 256], P('dom', 'hub'), may hold values from -6 to 6
Outputs:
- layer_out: bfloat16 [8, 4, 2048, 256], P('dom', 'hub')
- feats_grad: bfloat16 [8, 4, 2048, 256], P('dom', 'hub')
- grad_self: float32 [256, 256], replicated
- grad_neigh: float32 [256, 256], replicated
- grad_bias: float32 [256], replicated
- hub_grads: float32 [1024, 256], P('hub')
The draws below stay inside these ranges and needn't reach their ends.
Inputs may be any that keep to these rules, and one draw needn't show every extreme that they name: `send_rows`: entry [p, h, a, s] is a row of partition (p, h) that it sends to partition (a, h) in slot s; only the first send_counts[p, h, a] slots of a list are used. `send_counts`: a partition sends nothing to itself; each partition sends 32 rows to at least one peer and receives 32 rows from at least one peer.
All inputs are finite; a program needn't handle non-finite values.
Results may differ from the reference program's by a relative error of at most 0.0056.
Values may be sent and summed in bfloat16 or wider, within the bound.
A program may use at most 128 MiB of HBM per device.

```python
import math
import jax
import jax.numpy as jnp
import numpy as np
from jax import lax

WIDTH = 256
TILE = 128
KL = 3
KB = 2
KH = 2
ROWS = 2048
CAP = 32
PEERS = 8
LOOP = 4
BLOCKS = 16
HALO_BLOCKS = 2
HUB_BLOCKS = 8
HUB_ROWS = 1024
NODES = 65536


def draw_send_counts(key, part):
    shift_key = jax.random.fold_in(key, 11)
    offset_key = jax.random.fold_in(key, 12)
    shape_all = (PEERS, LOOP, PEERS)
    divisor = jax.random.randint(shift_key, shape_all, 1, 5)
    reduced = jnp.maximum(CAP // divisor, 1)
    offset = jax.random.randint(offset_key, (), 1, PEERS)
    source = lax.broadcasted_iota(jnp.int32, shape_all, 0)
    target = lax.broadcasted_iota(jnp.int32, shape_all, 2)
    full_peer = (source + offset) % PEERS
    counts = jnp.where(target == full_peer, CAP, reduced)
    return jnp.where(target == source, 0, counts).astype(jnp.int32)


def draw_send_rows(key, part):
    start_key = jax.random.fold_in(key, 21)
    step_key = jax.random.fold_in(key, 22)
    shape_all = (PEERS, LOOP, PEERS, 1)
    first_row = jax.random.randint(start_key, shape_all, 0, ROWS)
    stride = 2 * jax.random.randint(step_key, shape_all, 0, ROWS // 2) + 1
    slot_pos = lax.broadcasted_iota(jnp.int32, (PEERS, LOOP, PEERS, CAP), 3)
    return ((first_row + slot_pos * stride) % ROWS).astype(jnp.int32)


def set_ends(entries, key, smallest, largest):
    place = [jax.random.randint(jax.random.fold_in(key, axis), (), 0, length) for axis, length in enumerate(entries.shape)]
    widest = entries.shape.index(max(entries.shape))
    beside = place[:widest] + [(place[widest] + 1) % entries.shape[widest]] + place[widest + 1:]
    return entries.at[tuple(place)].set(smallest).at[tuple(beside)].set(largest)


def levels(key, extent, split, smallest, largest):
    level = 1.0
    for position, blocks in split:
        draws = jax.random.uniform(jax.random.fold_in(jax.random.fold_in(key, 6), position), (blocks,), jnp.float32, smallest / len(split), largest / len(split))
        level = level * jnp.repeat(jnp.exp(draws), extent[position] // blocks).reshape((-1,) + (1,) * (len(extent) - 1 - position))
    return level


def cumulative_ranks(number_of, skew):
    portions = [(1 << 20) // math.isqrt(rank ** skew) + 1 for rank in range(1, number_of + 1)]
    deviation = 1 + sum(portions) // (1 << 30)
    return np.cumsum(np.array([max(1, weight // deviation) for weight in portions]))


def ranked_ids(own_key, extent, number_of, lean):
    table = cumulative_ranks(number_of, lean)
    ticket = jax.random.randint(jax.random.fold_in(own_key, 1), extent, 0, int(table[number_of - 1]))
    standing = jnp.searchsorted(jnp.asarray(table, jnp.int32), ticket, side="right")
    return jax.random.permutation(jax.random.fold_in(own_key, 2), number_of)[standing].astype(jnp.int32)


def noise(key, dims, deviation, most, split=(), held_as=jnp.bfloat16):
    loudness = levels(key, dims, split, -0.22, 0.18) if split else 1.0
    values = jax.random.normal(key, dims, jnp.float32) * deviation * loudness
    return jnp.minimum(jnp.maximum(values, -most), most).astype(held_as)


def setup_inputs(seed: int = 0) -> dict:
    key_of = jax.random.split(jax.random.key(seed), 16)
    node_feats = noise(key_of[0], (PEERS, LOOP, ROWS, WIDTH), 1.0, 6.0, ((0, 8), (1, 4)))
    hub_feats = noise(key_of[1], (HUB_ROWS, WIDTH), 1.0, 6.0, ((0, 4),))
    w_self = noise(key_of[2], (WIDTH, WIDTH), WIDTH ** -0.5, 0.375)
    w_neigh = noise(key_of[3], (WIDTH, WIDTH), WIDTH ** -0.5, 0.375)
    out_bias = noise(key_of[4], (WIDTH,), 0.5, 3.0, (), jnp.float32)
    send_rows = draw_send_rows(jax.random.fold_in(key_of[15], 71), 0)
    send_counts = draw_send_counts(jax.random.fold_in(key_of[15], 71), 0)
    local_ids = set_ends(jax.random.randint(key_of[7], (PEERS, LOOP, BLOCKS, KL), 0, BLOCKS), jax.random.fold_in(key_of[7], 1), 0, BLOCKS - 1).astype(jnp.int32)
    local_tiles = noise(key_of[8], (PEERS, LOOP, BLOCKS, KL, TILE, TILE), TILE ** -0.5, 0.5, ((0, 8), (1, 4)))
    halo_ids = set_ends(jax.random.randint(key_of[9], (PEERS, LOOP, BLOCKS, KB), 0, HALO_BLOCKS), jax.random.fold_in(key_of[9], 1), 0, HALO_BLOCKS - 1).astype(jnp.int32)
    halo_tiles = noise(key_of[10], (PEERS, LOOP, BLOCKS, KB, TILE, TILE), TILE ** -0.5, 0.5, ((0, 8), (1, 4)))
    hub_ids = set_ends(ranked_ids(key_of[11], (PEERS, LOOP, BLOCKS, KH), HUB_BLOCKS, 2), jax.random.fold_in(key_of[11], 3), 0, HUB_BLOCKS - 1).astype(jnp.int32)
    hub_tiles = noise(key_of[12], (PEERS, LOOP, BLOCKS, KH, TILE, TILE), TILE ** -0.5, 0.5, ((0, 8), (1, 4)))
    degree = set_ends(jax.random.randint(key_of[13], (PEERS, LOOP, ROWS), 1, 9), jax.random.fold_in(key_of[13], 1), 1, 8).astype(jnp.int32)
    out_grad = noise(key_of[14], (PEERS, LOOP, ROWS, WIDTH), 1.0, 6.0, ((0, 8), (1, 4)))
    return dict(node_feats=node_feats, hub_feats=hub_feats, w_self=w_self, w_neigh=w_neigh, out_bias=out_bias, send_rows=send_rows, send_counts=send_counts, local_ids=local_ids, local_tiles=local_tiles, halo_ids=halo_ids, halo_tiles=halo_tiles, hub_ids=hub_ids, hub_tiles=hub_tiles, degree=degree, out_grad=out_grad)


def block_apply(tile_set, sources):
    return jnp.einsum('bkij,bkjf->bif', tile_set.astype(jnp.float32), sources.astype(jnp.float32))

def block_spread(tile_set, grad_blocks):
    return jnp.einsum('bkij,bif->bkjf', tile_set.astype(jnp.float32), grad_blocks.astype(jnp.float32))

def silu_slope(preact):
    sigmoid = jax.nn.sigmoid(preact)
    return sigmoid * (1.0 + preact * (1.0 - sigmoid))

def pick_rows(own_rows, index_rows):
    return own_rows[index_rows]

def add_back(own_rows, index_rows, values):
    return own_rows.at[index_rows.reshape(-1)].add(values.reshape(-1, WIDTH))

def reference(node_feats, hub_feats, w_self, w_neigh, out_bias, send_rows, send_counts, local_ids, local_tiles, halo_ids, halo_tiles, hub_ids, hub_tiles, degree, out_grad):
    slot_index = jnp.arange(CAP).astype(jnp.int32)
    send_live = slot_index[None, None, None, :] < send_counts[:, :, :, None]
    picked = jax.vmap(jax.vmap(pick_rows))(node_feats, send_rows)
    picked = jnp.where(send_live[..., None], picked, jnp.zeros((), picked.dtype))
    halo_all = jnp.transpose(picked, (2, 1, 0, 3, 4)).reshape(PEERS * LOOP, PEERS * CAP, WIDTH)
    hub_blocks = hub_feats.reshape(HUB_BLOCKS, TILE, WIDTH)

    def one_part(carried, inputs):
        sum_self, sum_neigh, sum_bias, sum_hub = carried
        features, halo_rows, local_index, local_tile, halo_index, halo_tile, hub_index, hub_tile, row_degree, grad_rows = inputs
        feat_blocks = features.reshape(BLOCKS, TILE, WIDTH)
        halo_blocks = halo_rows.reshape(HALO_BLOCKS, TILE, WIDTH)
        summed = block_apply(local_tile, feat_blocks[local_index])
        summed = summed + block_apply(halo_tile, halo_blocks[halo_index])
        summed = summed + block_apply(hub_tile, hub_blocks[hub_index])
        row_scale = 1.0 / row_degree.astype(jnp.float32)
        aggregate = (summed.reshape(ROWS, WIDTH) * row_scale[:, None]).astype(jnp.bfloat16)
        preact = jnp.dot(features, w_self, preferred_element_type=jnp.float32) + jnp.dot(aggregate, w_neigh, preferred_element_type=jnp.float32) + out_bias
        layer_rows = jax.nn.silu(preact).astype(jnp.bfloat16)
        grad_pre = (grad_rows.astype(jnp.float32) * silu_slope(preact)).astype(jnp.bfloat16)
        sum_self = sum_self + jnp.dot(features.T, grad_pre, preferred_element_type=jnp.float32)
        sum_neigh = sum_neigh + jnp.dot(aggregate.T, grad_pre, preferred_element_type=jnp.float32)
        sum_bias = sum_bias + lax.optimization_barrier(jnp.sum(grad_pre.astype(jnp.float32), axis=0))
        direct = jnp.dot(grad_pre, w_self.T, preferred_element_type=jnp.float32)
        grad_scaled = (jnp.dot(grad_pre, w_neigh.T, preferred_element_type=jnp.float32) * row_scale[:, None]).astype(jnp.bfloat16)
        grad_scaled = grad_scaled.reshape(BLOCKS, TILE, WIDTH)
        local_back = jax.ops.segment_sum(block_spread(local_tile, grad_scaled).reshape(BLOCKS * KL, TILE, WIDTH), local_index.reshape(-1), num_segments=BLOCKS)
        halo_back = jax.ops.segment_sum(block_spread(halo_tile, grad_scaled).reshape(BLOCKS * KB, TILE, WIDTH), halo_index.reshape(-1), num_segments=HALO_BLOCKS)
        hub_back = jax.ops.segment_sum(block_spread(hub_tile, grad_scaled).reshape(BLOCKS * KH, TILE, WIDTH), hub_index.reshape(-1), num_segments=HUB_BLOCKS)
        own_grad = direct + local_back.reshape(ROWS, WIDTH)
        sum_hub = sum_hub + hub_back.reshape(HUB_ROWS, WIDTH)
        return ((sum_self, sum_neigh, sum_bias, sum_hub), (layer_rows, own_grad, halo_back.reshape(PEERS, CAP, WIDTH)))
    parts_total = PEERS * LOOP
    inputs = (node_feats.reshape(parts_total, ROWS, WIDTH), halo_all, local_ids.reshape(parts_total, BLOCKS, KL), local_tiles.reshape(parts_total, BLOCKS, KL, TILE, TILE), halo_ids.reshape(parts_total, BLOCKS, KB), halo_tiles.reshape(parts_total, BLOCKS, KB, TILE, TILE), hub_ids.reshape(parts_total, BLOCKS, KH), hub_tiles.reshape(parts_total, BLOCKS, KH, TILE, TILE), degree.reshape(parts_total, ROWS), out_grad.reshape(parts_total, ROWS, WIDTH))
    initial = (jnp.zeros((WIDTH, WIDTH), jnp.float32), jnp.zeros((WIDTH, WIDTH), jnp.float32), jnp.zeros((WIDTH,), jnp.float32), jnp.zeros((HUB_ROWS, WIDTH), jnp.float32))
    totals, stacked = lax.scan(one_part, initial, inputs)
    sum_self, sum_neigh, sum_bias, sum_hub = totals
    layer_rows, own_grad, halo_back = stacked
    layer_out = layer_rows.reshape(PEERS, LOOP, ROWS, WIDTH)
    returned = jnp.transpose(halo_back.reshape(PEERS, LOOP, PEERS, CAP, WIDTH), (2, 1, 0, 3, 4))
    returned = jnp.where(send_live[..., None], returned, jnp.zeros((), returned.dtype))
    feats_grad = jax.vmap(jax.vmap(add_back))(own_grad.reshape(PEERS, LOOP, ROWS, WIDTH), send_rows, returned).astype(jnp.bfloat16)
    factor = 1.0 / math.sqrt(NODES)
    return (layer_out, feats_grad, sum_self * factor, sum_neigh * factor, sum_bias * factor, sum_hub)
```

```python
import functools
import math

import jax
import jax.numpy as jnp
from jax import lax
from jax.experimental import pallas as pl
from jax.experimental.pallas import tpu as pltpu
from jax.sharding import PartitionSpec as P

F32 = jnp.float32
BF16 = jnp.bfloat16
MESH = pl.DeviceIdType.MESH
VMEM_SPEC = pl.BlockSpec(memory_space=pltpu.VMEM)
VMEM_LIMIT = 48 * 1024 * 1024


def rows_at(index, size):
    return pl.ds(pl.multiple_of(index * size, size), size)


def greet(dom_size, hub_size, dom, hub):
    barrier = pltpu.get_barrier_semaphore()
    for off in range(1, hub_size):
        pl.semaphore_signal(
            barrier, inc=1, device_id=(dom, lax.rem(hub + off, hub_size)), device_id_type=MESH
        )
    for off in range(1, dom_size):
        pl.semaphore_signal(
            barrier, inc=1, device_id=(lax.rem(dom + off, dom_size), hub), device_id_type=MESH
        )
    return barrier


def remote(src, dst, send, recv, dom, hub):
    return pltpu.make_async_remote_copy(
        src_ref=src,
        dst_ref=dst,
        send_sem=send,
        recv_sem=recv,
        device_id=(dom, hub),
        device_id_type=MESH,
    )


def exchange_kernel(
    dom_size,
    hub_size,
    index_ref,
    feats_ref,
    hub_ref,
    halo_ref,
    hub_all_ref,
    outgoing,
    hub_send,
    hub_recv,
    dom_send,
    dom_recv,
):
    dom = lax.axis_index("dom")
    hub = lax.axis_index("hub")
    barrier = greet(dom_size, hub_size, dom, hub)
    row_count = feats_ref.shape[0]
    hub_rows = hub_ref.shape[0]
    slots = index_ref.shape[1]
    cap = slots // dom_size
    hub_all_ref[rows_at(hub, hub_rows), :] = hub_ref[...]
    pl.semaphore_wait(barrier, hub_size + dom_size - 2)
    copies = []
    for off in range(1, hub_size):
        copies.append(
            remote(
                hub_ref,
                hub_all_ref.at[rows_at(hub, hub_rows)],
                hub_send.at[off],
                hub_recv.at[off],
                dom,
                lax.rem(hub + off, hub_size),
            )
        )
        copies[-1].start()
    for part in range(slots // 128):
        wanted = jnp.broadcast_to(
            index_ref[:, part * 128 : (part + 1) * 128].astype(F32), (128, 128)
        ).T
        lane = lax.broadcasted_iota(jnp.int32, (128, 128), 1).astype(F32)
        onehot = jnp.concatenate(
            [
                (wanted == lane + float(start)).astype(F32).astype(BF16)
                for start in range(0, row_count, 128)
            ],
            axis=1,
        )
        outgoing[part * 128 : (part + 1) * 128, :] = jnp.dot(
            onehot, feats_ref[...], preferred_element_type=F32
        ).astype(BF16)
    for off in range(1, dom_size):
        target = lax.rem(dom + off, dom_size)
        copies.append(
            remote(
                outgoing.at[rows_at(target, cap)],
                halo_ref.at[rows_at(dom, cap)],
                dom_send.at[off],
                dom_recv.at[off],
                target,
                hub,
            )
        )
        copies[-1].start()
    halo_ref[rows_at(dom, cap), :] = outgoing[rows_at(dom, cap), :]
    for copy in copies:
        copy.wait()


def layer_kernel(
    span,
    hub_size,
    weight_rows,
    local_ids,
    halo_ids,
    hub_ids,
    feats_ref,
    halo_ref,
    hub_ref,
    local_tiles,
    halo_tiles,
    hub_tiles,
    degree_ref,
    out_grad_ref,
    w_self_ref,
    w_neigh_ref,
    bias_ref,
    layer_ref,
    own_ref,
    halo_back_ref,
    payload_ref,
    bias_part_ref,
    halo_acc,
    hub_acc,
    weight_acc,
    bias_acc,
):
    step = pl.program_id(0)
    width = feats_ref.shape[1]

    @pl.when(step == 0)
    def _():
        own_ref[...] = jnp.zeros_like(own_ref)
        halo_acc[...] = jnp.zeros_like(halo_acc)
        hub_acc[...] = jnp.zeros_like(hub_acc)
        weight_acc[...] = jnp.zeros_like(weight_acc)
        bias_acc[...] = jnp.zeros_like(bias_acc)

    groups = (
        (local_ids, local_tiles, feats_ref, own_ref),
        (halo_ids, halo_tiles, halo_ref, halo_acc),
        (hub_ids, hub_tiles, hub_ref, hub_acc),
    )
    features = feats_ref[rows_at(step, span * 128), :]
    scales = []
    sums = []
    for sub in range(span):
        block = step * span + sub
        scale = 1.0 / degree_ref[pl.ds(block, 1), :].astype(F32)
        scale = jnp.broadcast_to(scale, (128, 128)).T
        scales.append(jnp.concatenate([scale] * (width // 128), axis=1))
        tiles = []
        sources = []
        for ids, tile_ref, source_ref, _ in groups:
            for k in range(tile_ref.shape[1]):
                tiles.append(tile_ref[sub, k])
                sources.append(source_ref[rows_at(ids[block, k], 128), :])
        total = jnp.dot(
            jnp.concatenate(tiles, axis=1),
            jnp.concatenate(sources, axis=0),
            preferred_element_type=F32,
        )
        sums.append((total * scales[-1]).astype(BF16))
    aggregate = jnp.concatenate(sums, axis=0)
    preact = (
        jnp.dot(features, w_self_ref[...], preferred_element_type=F32)
        + jnp.dot(aggregate, w_neigh_ref[...], preferred_element_type=F32)
        + bias_ref[...]
    )
    sigmoid = 1.0 / (1.0 + jnp.exp(-preact))
    layer_ref[...] = (preact * sigmoid).astype(BF16)
    grad_wide = out_grad_ref[...].astype(F32) * (sigmoid * (1.0 + preact * (1.0 - sigmoid)))
    grad_pre = grad_wide.astype(BF16)
    bias_acc[...] += jnp.sum(
        grad_pre.astype(F32).reshape(span * 16, 8, width), axis=0
    )
    contract_rows = (((0,), (0,)), ((), ()))
    contract_cols = (((1,), (1,)), ((), ()))
    weight_acc[...] += lax.dot_general(
        jnp.concatenate([features, aggregate], axis=1),
        grad_pre,
        contract_rows,
        preferred_element_type=F32,
    )
    own_ref[rows_at(step, span * 128), :] += lax.dot_general(
        grad_pre, w_self_ref[...], contract_cols, preferred_element_type=F32
    )
    back = lax.dot_general(grad_pre, w_neigh_ref[...], contract_cols, preferred_element_type=F32)
    for sub in range(span):
        block = step * span + sub
        scaled = (back[sub * 128 : (sub + 1) * 128, :] * scales[sub]).astype(BF16)
        for ids, tile_ref, _, acc_ref in groups:
            for k in range(tile_ref.shape[1]):
                acc_ref[rows_at(ids[block, k], 128), :] += lax.dot_general(
                    tile_ref[sub, k], scaled, contract_rows, preferred_element_type=F32
                )

    @pl.when(step == pl.num_programs(0) - 1)
    def _():
        halo_back_ref[...] = halo_acc[...].astype(BF16)
        hub_rows = hub_acc.shape[0] // hub_size
        chunk = payload_ref.shape[1]
        for peer in range(hub_size):
            payload_ref[peer, :weight_rows, :] = weight_acc[
                peer * weight_rows : (peer + 1) * weight_rows, :
            ].astype(BF16)
            payload_ref[peer, weight_rows : weight_rows + hub_rows, :] = hub_acc[
                peer * hub_rows : (peer + 1) * hub_rows, :
            ].astype(BF16)
            if weight_rows + hub_rows < chunk:
                payload_ref[peer, weight_rows + hub_rows :, :] = jnp.zeros(
                    (chunk - weight_rows - hub_rows, width), BF16
                )
        bias_part_ref[...] = bias_acc[...]


def reduce_kernel(
    dom_size,
    hub_size,
    weight_rows,
    factor,
    index_ref,
    own_ref,
    halo_back_ref,
    payload_ref,
    bias_part_ref,
    feats_grad_ref,
    self_ref,
    neigh_ref,
    bias_out_ref,
    hub_out_ref,
    returned,
    hub_land,
    partial,
    dom_land,
    gathered,
    weights,
    bias_hub,
    bias_dom,
    hub_send,
    hub_recv,
    bias_hub_send,
    bias_hub_recv,
    back_send,
    back_recv,
    dom_send,
    dom_recv,
    bias_dom_send,
    bias_dom_recv,
    gather_send,
    gather_recv,
    weight_send,
    weight_recv,
):
    dom = lax.axis_index("dom")
    hub = lax.axis_index("hub")
    slots = index_ref.shape[1]
    cap = slots // dom_size
    chunk = payload_ref.shape[1]
    piece = chunk // dom_size
    width = own_ref.shape[1]
    barrier = greet(dom_size, hub_size, dom, hub)
    bias_hub[hub] = bias_part_ref[...]
    returned[rows_at(dom, cap), :] = halo_back_ref[rows_at(dom, cap), :]
    pl.semaphore_wait(barrier, hub_size + dom_size - 2)

    hub_copies = []
    for off in range(1, hub_size):
        target = lax.rem(hub + off, hub_size)
        hub_copies.append(
            remote(
                payload_ref.at[target],
                hub_land.at[off],
                hub_send.at[off],
                hub_recv.at[off],
                dom,
                target,
            )
        )
        hub_copies.append(
            remote(
                bias_part_ref,
                bias_hub.at[hub],
                bias_hub_send.at[off],
                bias_hub_recv.at[off],
                dom,
                target,
            )
        )
    for copy in hub_copies:
        copy.start()
    back_copies = []
    for off in range(1, dom_size):
        target = lax.rem(dom + off, dom_size)
        back_copies.append(
            remote(
                halo_back_ref.at[rows_at(target, cap)],
                returned.at[rows_at(dom, cap)],
                back_send.at[off],
                back_recv.at[off],
                target,
                hub,
            )
        )
        back_copies[-1].start()
    for copy in hub_copies:
        copy.wait()
    total = payload_ref[hub].astype(F32)
    for off in range(1, hub_size):
        total = total + hub_land[off].astype(F32)
    partial[...] = total.astype(BF16)
    bias_total = bias_hub[0]
    for peer in range(1, hub_size):
        bias_total = bias_total + bias_hub[peer]
    bias_dom[dom] = bias_total

    dom_copies = []
    for off in range(1, dom_size):
        target = lax.rem(dom + off, dom_size)
        dom_copies.append(
            remote(
                partial.at[rows_at(target, piece)],
                dom_land.at[off],
                dom_send.at[off],
                dom_recv.at[off],
                target,
                hub,
            )
        )
        dom_copies.append(
            remote(
                bias_dom.at[dom],
                bias_dom.at[dom],
                bias_dom_send.at[off],
                bias_dom_recv.at[off],
                target,
                hub,
            )
        )
    for copy in dom_copies:
        copy.start()
    for copy in dom_copies:
        copy.wait()
    total = partial[rows_at(dom, piece), :].astype(F32)
    for off in range(1, dom_size):
        total = total + dom_land[off].astype(F32)
    gathered[rows_at(dom, piece), :] = total.astype(BF16)
    gather_copies = []
    for off in range(1, dom_size):
        gather_copies.append(
            remote(
                gathered.at[rows_at(dom, piece)],
                gathered.at[rows_at(dom, piece)],
                gather_send.at[off],
                gather_recv.at[off],
                lax.rem(dom + off, dom_size),
                hub,
            )
        )
        gather_copies[-1].start()
    bias_total = bias_dom[0]
    for peer in range(1, dom_size):
        bias_total = bias_total + bias_dom[peer]
    bias_out_ref[...] = jnp.sum(bias_total, axis=0, keepdims=True) * factor

    for copy in back_copies:
        copy.wait()
    row_count = own_ref.shape[0]

    def add_back(step, carry):
        rows = rows_at(step, 256)
        row = lax.broadcasted_iota(jnp.int32, (256, slots), 0) + step * 256
        onehot = (row == index_ref[...]).astype(F32).astype(BF16)
        feats_grad_ref[rows, :] = (
            own_ref[rows, :] + jnp.dot(onehot, returned[...], preferred_element_type=F32)
        ).astype(BF16)
        return carry

    lax.fori_loop(0, row_count // 256, add_back, 0)

    for copy in gather_copies:
        copy.wait()
    weight_copies = []
    weights[hub] = gathered[:weight_rows, :]
    for off in range(1, hub_size):
        weight_copies.append(
            remote(
                gathered.at[pl.ds(0, weight_rows)],
                weights.at[hub],
                weight_send.at[off],
                weight_recv.at[off],
                dom,
                lax.rem(hub + off, hub_size),
            )
        )
        weight_copies[-1].start()
    hub_rows = hub_out_ref.shape[0]
    hub_out_ref[...] = gathered[weight_rows : weight_rows + hub_rows, :].astype(F32)
    for copy in weight_copies:
        copy.wait()
    half = hub_size // 2
    self_ref[...] = weights[:half].reshape(width, width).astype(F32) * factor
    neigh_ref[...] = weights[half:].reshape(width, width).astype(F32) * factor


def body(
    node_feats,
    hub_feats,
    w_self,
    w_neigh,
    out_bias,
    send_rows,
    send_counts,
    local_ids,
    local_tiles,
    halo_ids,
    halo_tiles,
    hub_ids,
    hub_tiles,
    degree,
    out_grad,
):
    dom_size = lax.axis_size("dom")
    hub_size = lax.axis_size("hub")
    rows, width = node_feats.shape[2:]
    tile = local_tiles.shape[-1]
    blocks = rows // tile
    cap = send_rows.shape[-1]
    slots = dom_size * cap
    hub_rows = hub_feats.shape[0]
    features = node_feats.reshape(rows, width)
    live = lax.broadcasted_iota(jnp.int32, (dom_size, cap), 1) < send_counts.reshape(dom_size, 1)
    index = jnp.where(live, send_rows.reshape(dom_size, cap), -1).reshape(1, slots)
    dma = pltpu.SemaphoreType.DMA

    halo, hub_all = pl.pallas_call(
        functools.partial(exchange_kernel, dom_size, hub_size),
        out_shape=(
            jax.ShapeDtypeStruct((slots, width), BF16),
            jax.ShapeDtypeStruct((hub_size * hub_rows, width), BF16),
        ),
        in_specs=[VMEM_SPEC] * 3,
        out_specs=(VMEM_SPEC,) * 2,
        scratch_shapes=[
            pltpu.VMEM((slots, width), BF16),
            dma((hub_size,)),
            dma((hub_size,)),
            dma((dom_size,)),
            dma((dom_size,)),
        ],
        compiler_params=pltpu.CompilerParams(
            collective_id=0, has_side_effects=True, vmem_limit_bytes=VMEM_LIMIT
        ),
        name="exchange",
    )(index, features, hub_feats)

    span = 2
    weight_rows = 2 * width // hub_size
    unit = 16 * dom_size
    chunk = (weight_rows + hub_rows + unit - 1) // unit * unit
    whole = lambda *shape: pl.BlockSpec(shape, lambda i, *_: (0,) * len(shape))
    tiles = lambda count: pl.BlockSpec((span, count, tile, tile), lambda i, *_: (i, 0, 0, 0))
    moving = pl.BlockSpec((span * tile, width), lambda i, *_: (i, 0))
    counts = (local_tiles.shape[3], halo_tiles.shape[3], hub_tiles.shape[3])
    layer_rows, own_grad, halo_back, payload, bias_part = pl.pallas_call(
        functools.partial(layer_kernel, span, hub_size, weight_rows),
        out_shape=(
            jax.ShapeDtypeStruct((rows, width), BF16),
            jax.ShapeDtypeStruct((rows, width), F32),
            jax.ShapeDtypeStruct((slots, width), BF16),
            jax.ShapeDtypeStruct((hub_size, chunk, width), BF16),
            jax.ShapeDtypeStruct((8, width), F32),
        ),
        grid_spec=pltpu.PrefetchScalarGridSpec(
            num_scalar_prefetch=3,
            grid=(blocks // span,),
            in_specs=[
                whole(rows, width),
                whole(slots, width),
                whole(hub_size * hub_rows, width),
                tiles(counts[0]),
                tiles(counts[1]),
                tiles(counts[2]),
                whole(blocks, tile),
                moving,
                whole(width, width),
                whole(width, width),
                whole(1, width),
            ],
            out_specs=(
                moving,
                whole(rows, width),
                whole(slots, width),
                whole(hub_size, chunk, width),
                whole(8, width),
            ),
            scratch_shapes=[
                pltpu.VMEM((slots, width), F32),
                pltpu.VMEM((hub_size * hub_rows, width), F32),
                pltpu.VMEM((2 * width, width), F32),
                pltpu.VMEM((8, width), F32),
            ],
        ),
        compiler_params=pltpu.CompilerParams(vmem_limit_bytes=VMEM_LIMIT),
        name="layer",
    )(
        local_ids.reshape(blocks, counts[0]),
        halo_ids.reshape(blocks, counts[1]),
        hub_ids.reshape(blocks, counts[2]),
        features,
        halo,
        hub_all,
        local_tiles.reshape(blocks, counts[0], tile, tile),
        halo_tiles.reshape(blocks, counts[1], tile, tile),
        hub_tiles.reshape(blocks, counts[2], tile, tile),
        degree.reshape(blocks, tile),
        out_grad.reshape(rows, width),
        w_self,
        w_neigh,
        out_bias.reshape(1, width),
    )

    factor = 1.0 / math.sqrt(rows * dom_size * hub_size)
    piece = chunk // dom_size
    feats_grad, grad_self, grad_neigh, grad_bias, hub_grads = pl.pallas_call(
        functools.partial(reduce_kernel, dom_size, hub_size, weight_rows, factor),
        out_shape=(
            jax.ShapeDtypeStruct((rows, width), BF16),
            jax.ShapeDtypeStruct((width, width), F32),
            jax.ShapeDtypeStruct((width, width), F32),
            jax.ShapeDtypeStruct((1, width), F32),
            jax.ShapeDtypeStruct((hub_rows, width), F32),
        ),
        in_specs=[VMEM_SPEC] * 5,
        out_specs=(VMEM_SPEC,) * 5,
        scratch_shapes=[
            pltpu.VMEM((slots, width), BF16),
            pltpu.VMEM((hub_size, chunk, width), BF16),
            pltpu.VMEM((chunk, width), BF16),
            pltpu.VMEM((dom_size, piece, width), BF16),
            pltpu.VMEM((chunk, width), BF16),
            pltpu.VMEM((hub_size, weight_rows, width), BF16),
            pltpu.VMEM((hub_size, 8, width), F32),
            pltpu.VMEM((dom_size, 8, width), F32),
            dma((hub_size,)),
            dma((hub_size,)),
            dma((hub_size,)),
            dma((hub_size,)),
            dma((dom_size,)),
            dma((dom_size,)),
            dma((dom_size,)),
            dma((dom_size,)),
            dma((dom_size,)),
            dma((dom_size,)),
            dma((dom_size,)),
            dma((dom_size,)),
            dma((hub_size,)),
            dma((hub_size,)),
        ],
        compiler_params=pltpu.CompilerParams(
            collective_id=1, has_side_effects=True, vmem_limit_bytes=VMEM_LIMIT
        ),
        name="reduce",
    )(index, own_grad, halo_back, payload, bias_part)
    return (
        layer_rows.reshape(node_feats.shape),
        feats_grad.reshape(node_feats.shape),
        grad_self,
        grad_neigh,
        grad_bias.reshape(width),
        hub_grads,
    )


def solution(mesh):
    placed = (
        P("dom", "hub", None, None),
        P("hub", None),
        P(),
        P(),
        P(),
        P("dom", "hub", None, None),
        P("dom", "hub", None),
        P("dom", "hub", None, None),
        P("dom", "hub", None, None, None, None),
        P("dom", "hub", None, None),
        P("dom", "hub", None, None, None, None),
        P("dom", "hub", None, None),
        P("dom", "hub", None, None, None, None),
        P("dom", "hub", None),
        P("dom", "hub", None, None),
    )
    return jax.shard_map(
        body,
        mesh=mesh,
        in_specs=placed,
        out_specs=(
            P("dom", "hub", None, None),
            P("dom", "hub", None, None),
            P(),
            P(),
            P(),
            P("hub", None),
        ),
        check_vma=False,
    )
```

```python
import functools
import math

import jax
import jax.numpy as jnp
from jax import lax
from jax.experimental import pallas as pl
from jax.experimental.pallas import tpu as pltpu
from jax.sharding import PartitionSpec as P

F32 = jnp.float32
BF16 = jnp.bfloat16
MESH = pl.DeviceIdType.MESH
VMEM_SPEC = pl.BlockSpec(memory_space=pltpu.VMEM)
VMEM_LIMIT = 60 * 1024 * 1024


def rows_at(index, size):
    return pl.ds(pl.multiple_of(index * size, size), size)


def greet(dom_size, hub_size, dom, hub):
    barrier = pltpu.get_barrier_semaphore()
    for off in range(1, hub_size):
        pl.semaphore_signal(
            barrier, inc=1, device_id=(dom, lax.rem(hub + off, hub_size)), device_id_type=MESH
        )
    for off in range(1, dom_size):
        pl.semaphore_signal(
            barrier, inc=1, device_id=(lax.rem(dom + off, dom_size), hub), device_id_type=MESH
        )
    return barrier


def remote(src, dst, send, recv, dom, hub):
    return pltpu.make_async_remote_copy(
        src_ref=src,
        dst_ref=dst,
        send_sem=send,
        recv_sem=recv,
        device_id=(dom, hub),
        device_id_type=MESH,
    )


def exchange_kernel(
    dom_size,
    hub_size,
    local_ids,
    rows_hbm,
    counts_hbm,
    feats_hbm,
    hub_hbm,
    tiles_hbm,
    halo_ref,
    hub_all_ref,
    column_ref,
    local_sum_ref,
    rows_in,
    counts_in,
    feats,
    tiles,
    index,
    outgoing,
    load_sem,
    hub_send,
    hub_recv,
    relay_send,
    relay_recv,
    dom_send,
    dom_recv,
):
    dom = lax.axis_index("dom")
    hub = lax.axis_index("hub")
    blocks, tile, width = feats.shape
    row_count = blocks * tile
    hub_rows = hub_hbm.shape[0]
    cap = rows_in.shape[1]
    line = hub_size // 2
    core = lax.rem(hub, 2)
    place = hub // 2
    sibling = hub + 1 - 2 * core
    loads = [
        pltpu.make_async_copy(source, target, load_sem.at[number])
        for number, (source, target) in enumerate(
            (
                (rows_hbm, rows_in),
                (counts_hbm, counts_in),
                (feats_hbm, feats),
                (hub_hbm, hub_all_ref.at[rows_at(hub, hub_rows)]),
                (tiles_hbm, tiles),
            )
        )
    ]
    for load in loads:
        load.start()
    barrier = greet(dom_size, hub_size, dom, hub)
    pl.semaphore_wait(barrier, hub_size + dom_size - 2)
    own_block = hub_all_ref.at[rows_at(hub, hub_rows)]
    hub_copies = []
    for off in range(line):
        target = sibling if off == 0 else lax.rem(place + off, line) * 2 + core
        hub_copies.append(
            remote(hub_hbm, own_block, hub_send.at[off], hub_recv.at[off], dom, target)
        )
    for copy in hub_copies[1:] + hub_copies[:1]:
        copy.start()
    for load in loads[:3]:
        load.wait()
    shape = (dom_size, dom_size)
    diagonal = lax.broadcasted_iota(jnp.int32, shape, 0) == lax.broadcasted_iota(
        jnp.int32, shape, 1
    )
    wide_counts = jnp.broadcast_to(counts_in[...].astype(F32), shape)
    count = jnp.sum(jnp.where(diagonal, wide_counts, 0.0), axis=1, keepdims=True)
    live = lax.broadcasted_iota(jnp.int32, (dom_size, cap), 1).astype(F32) < count
    index[...] = jnp.full((128, 128), -1.0, F32)
    index[:dom_size, :cap] = jnp.where(live, rows_in[...].astype(F32), -1.0)
    turned = index[...].T
    column = jnp.concatenate(
        [
            jnp.broadcast_to(turned[:cap, peer : peer + 1], (cap, 128))
            for peer in range(dom_size)
        ],
        axis=0,
    )
    column_ref[...] = column
    lane = lax.broadcasted_iota(jnp.int32, column.shape, 1).astype(F32)
    onehot = jnp.concatenate(
        [
            (column == lane + float(start)).astype(F32).astype(BF16)
            for start in range(0, row_count, 128)
        ],
        axis=1,
    )
    outgoing[...] = jnp.dot(
        onehot, feats[...].reshape(row_count, width), preferred_element_type=F32).astype(BF16)
    dom_copies = []
    for off in range(1, dom_size):
        target = lax.rem(dom + off, dom_size)
        dom_copies.append(
            remote(
                outgoing.at[rows_at(target, cap)],
                halo_ref.at[rows_at(dom, cap)],
                dom_send.at[off],
                dom_recv.at[off],
                target,
                hub,
            )
        )
        dom_copies[-1].start()
    halo_ref[rows_at(dom, cap), :] = outgoing[rows_at(dom, cap), :]
    for load in loads[3:]:
        load.wait()

    def local_sum(block, carry):
        taken = [tiles[block, k] for k in range(tiles.shape[1])]
        sources = [feats[local_ids[k, 0, block]] for k in range(tiles.shape[1])]
        local_sum_ref[rows_at(block, 128), :] = jnp.dot(
            jnp.concatenate(taken, axis=1),
            jnp.concatenate(sources, axis=0),
            preferred_element_type=F32,
        )
        return carry

    lax.fori_loop(0, blocks // 2, local_sum, 0)
    relays = []
    for off in range(1, line):
        hub_copies[off].wait()
        source = hub_all_ref.at[
            rows_at(lax.rem(place + line - off, line) * 2 + core, hub_rows)
        ]
        relays.append(
            remote(source, source, relay_send.at[off], relay_recv.at[off], dom, sibling)
        )
        relays[-1].start()
    lax.fori_loop(blocks // 2, blocks, local_sum, 0)
    for copy in hub_copies[:1] + relays + dom_copies:
        copy.wait()


def layer_kernel(
    span,
    hub_size,
    weight_rows,
    local_ids,
    halo_ids,
    hub_ids,
    feats_ref,
    local_sum_ref,
    halo_ref,
    hub_ref,
    local_tiles,
    halo_tiles,
    hub_tiles,
    degree_ref,
    out_grad_ref,
    w_self_ref,
    w_neigh_ref,
    bias_ref,
    layer_ref,
    own_ref,
    halo_back_ref,
    payload_ref,
    bias_part_ref,
    halo_acc,
    hub_acc,
    weight_acc,
    bias_acc,
):
    step = pl.program_id(0)
    width = feats_ref.shape[1]

    @pl.when(step == 0)
    def _():
        own_ref[...] = jnp.zeros_like(own_ref)
        halo_acc[...] = jnp.zeros_like(halo_acc)
        hub_acc[...] = jnp.zeros_like(hub_acc)
        weight_acc[...] = jnp.zeros_like(weight_acc)
        bias_acc[...] = jnp.zeros_like(bias_acc)

    groups = (
        (lambda k, block: local_ids[k, 0, block], local_tiles, None, own_ref),
        (lambda k, block: halo_ids[k, block], halo_tiles, halo_ref, halo_acc),
        (lambda k, block: hub_ids[k, block], hub_tiles, hub_ref, hub_acc),
    )
    features = feats_ref[...]
    scales = []
    sums = []
    for sub in range(span):
        block = step * span + sub
        scale = 1.0 / degree_ref[pl.ds(block, 1), :].astype(F32)
        scale = jnp.broadcast_to(scale, (128, 128)).T
        scales.append(jnp.concatenate([scale] * (width // 128), axis=1))
        tiles = []
        sources = []
        for ids, tile_ref, source_ref, _ in groups[1:]:
            for k in range(tile_ref.shape[1]):
                tiles.append(tile_ref[sub, k])
                sources.append(source_ref[rows_at(ids(k, block), 128), :])
        total = local_sum_ref[sub * 128 : (sub + 1) * 128, :] + jnp.dot(
            jnp.concatenate(tiles, axis=1),
            jnp.concatenate(sources, axis=0),
            preferred_element_type=F32,
        )
        sums.append((total * scales[-1]).astype(BF16))
    aggregate = jnp.concatenate(sums, axis=0)
    preact = (
        jnp.dot(features, w_self_ref[...], preferred_element_type=F32)
        + jnp.dot(aggregate, w_neigh_ref[...], preferred_element_type=F32)
        + bias_ref[...]
    )
    sigmoid = 1.0 / (1.0 + jnp.exp(-preact))
    layer_ref[...] = (preact * sigmoid).astype(BF16)
    grad_wide = out_grad_ref[...].astype(F32) * (sigmoid * (1.0 + preact * (1.0 - sigmoid)))
    grad_pre = grad_wide.astype(BF16)
    bias_acc[...] += jnp.sum(
        grad_pre.astype(F32).reshape(span * 16, 8, width), axis=0
    )
    contract_rows = (((0,), (0,)), ((), ()))
    contract_cols = (((1,), (1,)), ((), ()))
    weight_acc[...] += lax.dot_general(
        jnp.concatenate([features, aggregate], axis=1),
        grad_pre,
        contract_rows,
        preferred_element_type=F32,
    )
    own_ref[rows_at(step, span * 128), :] += lax.dot_general(
        grad_pre, w_self_ref[...], contract_cols, preferred_element_type=F32
    )
    back = lax.dot_general(grad_pre, w_neigh_ref[...], contract_cols, preferred_element_type=F32)
    for sub in range(span):
        block = step * span + sub
        scaled = (back[sub * 128 : (sub + 1) * 128, :] * scales[sub]).astype(BF16)
        for ids, tile_ref, _, acc_ref in groups:
            for k in range(tile_ref.shape[1]):
                acc_ref[rows_at(ids(k, block), 128), :] += lax.dot_general(
                    tile_ref[sub, k], scaled, contract_rows, preferred_element_type=F32
                )

    @pl.when(step == pl.num_programs(0) - 1)
    def _():
        halo_back_ref[...] = halo_acc[...].astype(BF16)
        hub_rows = hub_acc.shape[0] // hub_size
        pieces, line, unit = payload_ref.shape[1:4]
        for peer in range(hub_size):
            for piece in range(pieces):
                first = piece * unit
                parts = []
                if first < weight_rows:
                    end = min(first + unit, weight_rows)
                    base = peer * weight_rows
                    parts.append(weight_acc[base + first : base + end, :])
                low = max(first - weight_rows, 0)
                high = min(first + unit - weight_rows, hub_rows)
                if low < high:
                    base = peer * hub_rows
                    parts.append(hub_acc[base + low : base + high, :])
                rest = unit - sum(part.shape[0] for part in parts)
                if rest:
                    parts.append(jnp.zeros((rest, width), F32))
                at = 0
                for part in parts:
                    payload_ref[peer % 2, piece, peer // 2, at : at + part.shape[0], :] = part
                    at += part.shape[0]
        bias_part_ref[...] = bias_acc[...]


def reduce_kernel(
    dom_size,
    hub_size,
    weight_rows,
    factor,
    column_ref,
    own_hbm,
    halo_back_ref,
    payload_hbm,
    bias_part_ref,
    feats_grad_ref,
    self_ref,
    neigh_ref,
    bias_out_ref,
    hub_out_ref,
    own,
    returned,
    mine,
    core_land,
    line_out,
    line_land,
    held,
    partial,
    dom_land,
    gathered,
    weights,
    bias_hub,
    bias_dom,
    load_sem,
    core_send,
    core_recv,
    line_send,
    line_recv,
    bias_hub_send,
    bias_hub_recv,
    back_send,
    back_recv,
    dom_send,
    dom_recv,
    bias_dom_send,
    bias_dom_recv,
    gather_send,
    gather_recv,
    weight_send,
    weight_recv,
    relay_send,
    relay_recv,
):
    dom = lax.axis_index("dom")
    hub = lax.axis_index("hub")
    slots = column_ref.shape[0]
    cap = slots // dom_size
    pieces, line, unit, width = mine.shape
    share = unit // dom_size
    core = lax.rem(hub, 2)
    place = hub // 2
    sibling = hub + 1 - 2 * core
    loads = [
        pltpu.make_async_copy(payload_hbm.at[core], mine, load_sem.at[0]),
        pltpu.make_async_copy(own_hbm, own, load_sem.at[1]),
    ]
    for load in loads:
        load.start()
    barrier = greet(dom_size, hub_size, dom, hub)
    bias_hub[hub] = bias_part_ref[...]
    returned[rows_at(dom, cap), :] = halo_back_ref[rows_at(dom, cap), :]
    pl.semaphore_wait(barrier, hub_size + dom_size - 2)

    core_copies = []
    for q in range(pieces):
        core_copies.append(
            remote(
                payload_hbm.at[1 - core, q],
                core_land.at[q],
                core_send.at[q],
                core_recv.at[q],
                dom,
                sibling,
            )
        )
        core_copies[-1].start()
    bias_copies = []
    for off in range(1, hub_size):
        bias_copies.append(
            remote(
                bias_part_ref,
                bias_hub.at[hub],
                bias_hub_send.at[off],
                bias_hub_recv.at[off],
                dom,
                lax.rem(hub + off, hub_size),
            )
        )
        bias_copies[-1].start()
    back_copies = []
    for off in range(1, dom_size):
        target = lax.rem(dom + off, dom_size)
        back_copies.append(
            remote(
                halo_back_ref.at[rows_at(target, cap)],
                returned.at[rows_at(dom, cap)],
                back_send.at[off],
                back_recv.at[off],
                target,
                hub,
            )
        )
        back_copies[-1].start()
    loads[0].wait()
    line_copies = []
    for q in range(pieces):
        core_copies[q].wait()
        line_copies.append([])
        for off in range(1, line):
            target = lax.rem(place + off, line)
            line_out[q, off] = (mine[q, target] + core_land[q, target]).astype(BF16)
            copy = remote(
                line_out.at[q, off],
                line_land.at[q, off],
                line_send.at[q, off],
                line_recv.at[q, off],
                dom,
                target * 2 + core,
            )
            copy.start()
            line_copies[q].append(copy)
    for copy in bias_copies:
        copy.wait()
    bias_total = bias_hub[0]
    for peer in range(1, hub_size):
        bias_total = bias_total + bias_hub[peer]
    bias_dom[dom] = bias_total
    bias_copies = []
    for off in range(1, dom_size):
        bias_copies.append(
            remote(
                bias_dom.at[dom],
                bias_dom.at[dom],
                bias_dom_send.at[off],
                bias_dom_recv.at[off],
                lax.rem(dom + off, dom_size),
                hub,
            )
        )
        bias_copies[-1].start()
    dom_copies = []
    for q in range(pieces):
        total = mine[q, place] + core_land[q, place]
        for copy in line_copies[q]:
            copy.wait()
        for off in range(1, line):
            total = total + line_land[q, off].astype(F32)
        held[q] = total
        partial[q] = total.astype(BF16)
        dom_copies.append([])
        for off in range(1, dom_size):
            target = lax.rem(dom + off, dom_size)
            copy = remote(
                partial.at[q, rows_at(target, share)],
                dom_land.at[q, off],
                dom_send.at[q, off],
                dom_recv.at[q, off],
                target,
                hub,
            )
            copy.start()
            dom_copies[q].append(copy)
    gather_copies = []
    for q in range(pieces):
        for copy in dom_copies[q]:
            copy.wait()
        total = held[q, rows_at(dom, share), :]
        for off in range(1, dom_size):
            total = total + dom_land[q, off].astype(F32)
        gathered[q, rows_at(dom, share), :] = total.astype(BF16)
        gather_copies.append([])
        for off in range(1, dom_size):
            copy = remote(
                gathered.at[q, rows_at(dom, share)],
                gathered.at[q, rows_at(dom, share)],
                gather_send.at[q, off],
                gather_recv.at[q, off],
                lax.rem(dom + off, dom_size),
                hub,
            )
            copy.start()
            gather_copies[q].append(copy)

    for copy in gather_copies[0]:
        copy.wait()
    weights[hub] = gathered[0, :weight_rows, :]
    weight_copies = []
    for off in range(line):
        weight_copies.append(
            remote(
                gathered.at[0, pl.ds(0, weight_rows)],
                weights.at[hub],
                weight_send.at[off],
                weight_recv.at[off],
                dom,
                sibling if off == 0 else lax.rem(place + off, line) * 2 + core,
            )
        )
    for copy in weight_copies[1:] + weight_copies[:1]:
        copy.start()

    for copy in back_copies + bias_copies:
        copy.wait()
    loads[1].wait()
    bias_total = bias_dom[0]
    for peer in range(1, dom_size):
        bias_total = bias_total + bias_dom[peer]
    bias_out_ref[...] = jnp.sum(bias_total, axis=0, keepdims=True) * factor
    row_count = own.shape[0]

    def add_back(step, carry):
        rows = rows_at(step, 256)
        lane = lax.broadcasted_iota(jnp.int32, (slots, 256), 1) + step * 256
        wanted = jnp.concatenate([column_ref[...]] * 2, axis=1)
        onehot = (wanted == lane.astype(F32)).astype(F32).astype(BF16)
        feats_grad_ref[rows, :] = (
            own[rows, :]
            + lax.dot_general(
                onehot,
                returned[...],
                (((0,), (0,)), ((), ())),
                preferred_element_type=F32,
            )
        ).astype(BF16)
        return carry

    lax.fori_loop(0, row_count // 512, add_back, 0)
    relays = []
    for off in range(1, line):
        weight_copies[off].wait()
        source = weights.at[lax.rem(place + line - off, line) * 2 + core]
        relays.append(
            remote(source, source, relay_send.at[off], relay_recv.at[off], dom, sibling)
        )
        relays[-1].start()
    lax.fori_loop(row_count // 512, row_count // 256, add_back, 0)

    for copies in gather_copies[1:]:
        for copy in copies:
            copy.wait()
    hub_rows = hub_out_ref.shape[0]
    for q in range(pieces):
        low = max(q * unit, weight_rows)
        high = min((q + 1) * unit, weight_rows + hub_rows)
        if low < high:
            hub_out_ref[low - weight_rows : high - weight_rows, :] = gathered[
                q, low - q * unit : high - q * unit, :
            ].astype(F32)
    for copy in weight_copies[:1] + relays:
        copy.wait()
    half = hub_size // 2
    self_ref[...] = weights[:half].reshape(width, width).astype(F32) * factor
    neigh_ref[...] = weights[half:].reshape(width, width).astype(F32) * factor


def body(
    node_feats,
    hub_feats,
    w_self,
    w_neigh,
    out_bias,
    send_rows,
    send_counts,
    local_ids,
    local_tiles,
    halo_ids,
    halo_tiles,
    hub_ids,
    hub_tiles,
    degree,
    out_grad,
):
    dom_size = lax.axis_size("dom")
    hub_size = lax.axis_size("hub")
    rows, width = node_feats.shape[2:]
    tile = local_tiles.shape[-1]
    blocks = rows // tile
    cap = send_rows.shape[-1]
    slots = dom_size * cap
    hub_rows = hub_feats.shape[0]
    features = node_feats.reshape(rows, width)
    dma = pltpu.SemaphoreType.DMA
    any_spec = pl.BlockSpec(memory_space=pl.ANY)
    counts = (local_tiles.shape[3], halo_tiles.shape[3], hub_tiles.shape[3])
    local_sets = local_tiles.reshape(blocks, counts[0], tile, tile)
    local_table = jnp.transpose(local_ids, (0, 3, 1, 2)).reshape(counts[0], 1, blocks)
    halo_table = jnp.transpose(halo_ids, (0, 1, 3, 2)).reshape(counts[1], blocks)
    hub_table = jnp.transpose(hub_ids, (0, 1, 3, 2)).reshape(counts[2], blocks)
    line = hub_size // 2

    halo, hub_all, column, local_sum = pl.pallas_call(
        functools.partial(exchange_kernel, dom_size, hub_size),
        out_shape=(
            jax.ShapeDtypeStruct((slots, width), BF16),
            jax.ShapeDtypeStruct((hub_size * hub_rows, width), BF16),
            jax.ShapeDtypeStruct((slots, 128), F32),
            jax.ShapeDtypeStruct((rows, width), F32),
        ),
        in_specs=[pl.BlockSpec(memory_space=pltpu.SMEM)] + [any_spec] * 5,
        out_specs=(VMEM_SPEC,) * 4,
        scratch_shapes=[
            pltpu.VMEM((dom_size, cap), jnp.int32),
            pltpu.VMEM((1, dom_size), jnp.int32),
            pltpu.VMEM((blocks, tile, width), BF16),
            pltpu.VMEM((blocks, counts[0], tile, tile), BF16),
            pltpu.VMEM((128, 128), F32),
            pltpu.VMEM((slots, width), BF16),
            dma((5,)),
            dma((line,)),
            dma((line,)),
            dma((line,)),
            dma((line,)),
            dma((dom_size,)),
            dma((dom_size,)),
        ],
        compiler_params=pltpu.CompilerParams(
            collective_id=0, has_side_effects=True, vmem_limit_bytes=VMEM_LIMIT
        ),
        name="exchange",
    )(
        local_table,
        send_rows.reshape(dom_size, cap),
        send_counts.reshape(1, dom_size),
        node_feats.reshape(blocks, tile, width),
        hub_feats,
        local_sets,
    )

    span = 2
    weight_rows = 2 * width // hub_size
    unit = 16 * dom_size
    pieces = (weight_rows + hub_rows + unit - 1) // unit
    whole = lambda *shape: pl.BlockSpec(shape, lambda i, *_: (0,) * len(shape))
    tiles = lambda count: pl.BlockSpec((span, count, tile, tile), lambda i, *_: (i, 0, 0, 0))
    moving = pl.BlockSpec((span * tile, width), lambda i, *_: (i, 0))
    layer_rows, own_grad, halo_back, payload, bias_part = pl.pallas_call(
        functools.partial(layer_kernel, span, hub_size, weight_rows),
        out_shape=(
            jax.ShapeDtypeStruct((rows, width), BF16),
            jax.ShapeDtypeStruct((rows, width), F32),
            jax.ShapeDtypeStruct((slots, width), BF16),
            jax.ShapeDtypeStruct((2, pieces, line, unit, width), F32),
            jax.ShapeDtypeStruct((8, width), F32),
        ),
        grid_spec=pltpu.PrefetchScalarGridSpec(
            num_scalar_prefetch=3,
            grid=(blocks // span,),
            in_specs=[
                moving,
                moving,
                whole(slots, width),
                whole(hub_size * hub_rows, width),
                tiles(counts[0]),
                tiles(counts[1]),
                tiles(counts[2]),
                whole(blocks, tile),
                moving,
                whole(width, width),
                whole(width, width),
                whole(1, width),
            ],
            out_specs=(
                moving,
                whole(rows, width),
                whole(slots, width),
                whole(2, pieces, line, unit, width),
                whole(8, width),
            ),
            scratch_shapes=[
                pltpu.VMEM((slots, width), F32),
                pltpu.VMEM((hub_size * hub_rows, width), F32),
                pltpu.VMEM((2 * width, width), F32),
                pltpu.VMEM((8, width), F32),
            ],
        ),
        compiler_params=pltpu.CompilerParams(vmem_limit_bytes=VMEM_LIMIT),
        name="layer",
    )(
        local_table,
        halo_table,
        hub_table,
        features,
        local_sum,
        halo,
        hub_all,
        local_sets,
        halo_tiles.reshape(blocks, counts[1], tile, tile),
        hub_tiles.reshape(blocks, counts[2], tile, tile),
        degree.reshape(blocks, tile),
        out_grad.reshape(rows, width),
        w_self,
        w_neigh,
        out_bias.reshape(1, width),
    )

    factor = 1.0 / math.sqrt(rows * dom_size * hub_size)
    share = unit // dom_size
    pairs = [dma((pieces,))] * 2 + [dma((pieces, line))] * 2 + [dma((hub_size,))] * 2
    pairs += [dma((dom_size,))] * 2 + [dma((pieces, dom_size))] * 2 + [dma((dom_size,))] * 2
    pairs += [dma((pieces, dom_size))] * 2 + [dma((line,))] * 4
    feats_grad, grad_self, grad_neigh, grad_bias, hub_grads = pl.pallas_call(
        functools.partial(reduce_kernel, dom_size, hub_size, weight_rows, factor),
        out_shape=(
            jax.ShapeDtypeStruct((rows, width), BF16),
            jax.ShapeDtypeStruct((width, width), F32),
            jax.ShapeDtypeStruct((width, width), F32),
            jax.ShapeDtypeStruct((1, width), F32),
            jax.ShapeDtypeStruct((hub_rows, width), F32),
        ),
        in_specs=[VMEM_SPEC, any_spec, VMEM_SPEC, any_spec, VMEM_SPEC],
        out_specs=(VMEM_SPEC,) * 5,
        scratch_shapes=[
            pltpu.VMEM((rows, width), F32),
            pltpu.VMEM((slots, width), BF16),
            pltpu.VMEM((pieces, line, unit, width), F32),
            pltpu.VMEM((pieces, line, unit, width), F32),
            pltpu.VMEM((pieces, line, unit, width), BF16),
            pltpu.VMEM((pieces, line, unit, width), BF16),
            pltpu.VMEM((pieces, unit, width), F32),
            pltpu.VMEM((pieces, unit, width), BF16),
            pltpu.VMEM((pieces, dom_size, share, width), BF16),
            pltpu.VMEM((pieces, unit, width), BF16),
            pltpu.VMEM((hub_size, weight_rows, width), BF16),
            pltpu.VMEM((hub_size, 8, width), F32),
            pltpu.VMEM((dom_size, 8, width), F32),
            dma((2,)),
        ]
        + pairs,
        compiler_params=pltpu.CompilerParams(
            collective_id=1, has_side_effects=True, vmem_limit_bytes=VMEM_LIMIT
        ),
        name="reduce",
    )(column, own_grad, halo_back, payload, bias_part)
    return (
        layer_rows.reshape(node_feats.shape),
        feats_grad.reshape(node_feats.shape),
        grad_self,
        grad_neigh,
        grad_bias.reshape(width),
        hub_grads,
    )


def solution(mesh):
    placed = (
        P("dom", "hub", None, None),
        P("hub", None),
        P(),
        P(),
        P(),
        P("dom", "hub", None, None),
        P("dom", "hub", None),
        P("dom", "hub", None, None),
        P("dom", "hub", None, None, None, None),
        P("dom", "hub", None, None),
        P("dom", "hub", None, None, None, None),
        P("dom", "hub", None, None),
        P("dom", "hub", None, None, None, None),
        P("dom", "hub", None),
        P("dom", "hub", None, None),
    )
    return jax.shard_map(
        body,
        mesh=mesh,
        in_specs=placed,
        out_specs=(
            P("dom", "hub", None, None),
            P("dom", "hub", None, None),
            P(),
            P(),
            P(),
            P("hub", None),
        ),
        check_vma=False,
    )
```

```python
import functools
import math

import jax
import jax.numpy as jnp
from jax import lax
from jax.experimental import pallas as pl
from jax.experimental.pallas import tpu as pltpu
from jax.sharding import PartitionSpec as P

F32 = jnp.float32
BF16 = jnp.bfloat16
MESH = pl.DeviceIdType.MESH
VMEM_SPEC = pl.BlockSpec(memory_space=pltpu.VMEM)
VMEM_LIMIT = 60 * 1024 * 1024


def rows_at(index, size):
    return pl.ds(pl.multiple_of(index * size, size), size)


def greet(dom_size, hub_size, dom, hub):
    barrier = pltpu.get_barrier_semaphore()
    for off in range(1, hub_size):
        pl.semaphore_signal(
            barrier, inc=1, device_id=(dom, lax.rem(hub + off, hub_size)), device_id_type=MESH
        )
    for off in range(1, dom_size):
        pl.semaphore_signal(
            barrier, inc=1, device_id=(lax.rem(dom + off, dom_size), hub), device_id_type=MESH
        )
    return barrier


def remote(src, dst, send, recv, dom, hub):
    return pltpu.make_async_remote_copy(
        src_ref=src,
        dst_ref=dst,
        send_sem=send,
        recv_sem=recv,
        device_id=(dom, hub),
        device_id_type=MESH,
    )


def exchange_kernel(
    dom_size,
    hub_size,
    local_ids,
    rows_hbm,
    counts_hbm,
    feats_hbm,
    hub_hbm,
    tiles_hbm,
    halo_ref,
    hub_all_ref,
    column_ref,
    local_sum_ref,
    rows_in,
    counts_in,
    feats,
    tiles,
    index,
    outgoing,
    load_sem,
    hub_send,
    hub_recv,
    relay_send,
    relay_recv,
    dom_send,
    dom_recv,
):
    dom = lax.axis_index("dom")
    hub = lax.axis_index("hub")
    blocks, tile, width = feats.shape
    row_count = blocks * tile
    hub_rows = hub_hbm.shape[0]
    cap = rows_in.shape[1]
    line = hub_size // 2
    core = lax.rem(hub, 2)
    place = hub // 2
    sibling = hub + 1 - 2 * core
    loads = [
        pltpu.make_async_copy(source, target, load_sem.at[number])
        for number, (source, target) in enumerate(
            (
                (rows_hbm, rows_in),
                (counts_hbm, counts_in),
                (feats_hbm, feats),
                (hub_hbm, hub_all_ref.at[rows_at(hub, hub_rows)]),
                (tiles_hbm, tiles),
            )
        )
    ]
    for load in loads:
        load.start()
    barrier = greet(dom_size, hub_size, dom, hub)
    pl.semaphore_wait(barrier, hub_size + dom_size - 2)
    own_block = hub_all_ref.at[rows_at(hub, hub_rows)]
    hub_copies = []
    for off in range(line):
        target = sibling if off == 0 else lax.rem(place + off, line) * 2 + core
        hub_copies.append(
            remote(hub_hbm, own_block, hub_send.at[off], hub_recv.at[off], dom, target)
        )
    for copy in hub_copies[1:] + hub_copies[:1]:
        copy.start()
    for load in loads[:3]:
        load.wait()
    shape = (dom_size, dom_size)
    diagonal = lax.broadcasted_iota(jnp.int32, shape, 0) == lax.broadcasted_iota(
        jnp.int32, shape, 1
    )
    wide_counts = jnp.broadcast_to(counts_in[...].astype(F32), shape)
    count = jnp.sum(jnp.where(diagonal, wide_counts, 0.0), axis=1, keepdims=True)
    live = lax.broadcasted_iota(jnp.int32, (dom_size, cap), 1).astype(F32) < count
    index[...] = jnp.full((128, 128), -1.0, F32)
    index[:dom_size, :cap] = jnp.where(live, rows_in[...].astype(F32), -1.0)
    turned = index[...].T
    column = jnp.concatenate(
        [
            jnp.broadcast_to(turned[:cap, peer : peer + 1], (cap, 128))
            for peer in range(dom_size)
        ],
        axis=0,
    )
    column_ref[...] = column.T[:8, :]
    lane = lax.broadcasted_iota(jnp.int32, column.shape, 1).astype(F32)
    onehot = jnp.concatenate(
        [
            (column == lane + float(start)).astype(F32).astype(BF16)
            for start in range(0, row_count, 128)
        ],
        axis=1,
    )
    outgoing[...] = jnp.dot(
        onehot, feats[...].reshape(row_count, width), preferred_element_type=F32).astype(BF16)
    dom_copies = []
    for off in range(1, dom_size):
        target = lax.rem(dom + off, dom_size)
        dom_copies.append(
            remote(
                outgoing.at[rows_at(target, cap)],
                halo_ref.at[rows_at(dom, cap)],
                dom_send.at[off],
                dom_recv.at[off],
                target,
                hub,
            )
        )
        dom_copies[-1].start()
    halo_ref[rows_at(dom, cap), :] = outgoing[rows_at(dom, cap), :]
    for load in loads[3:]:
        load.wait()

    def local_sum(block, carry):
        taken = [tiles[block, k] for k in range(tiles.shape[1])]
        sources = [feats[local_ids[k, 0, block]] for k in range(tiles.shape[1])]
        local_sum_ref[rows_at(block, 128), :] = jnp.dot(
            jnp.concatenate(taken, axis=1),
            jnp.concatenate(sources, axis=0),
            preferred_element_type=F32,
        )
        return carry

    lax.fori_loop(0, blocks // 2, local_sum, 0)
    relays = []
    for off in range(1, line):
        hub_copies[off].wait()
        source = hub_all_ref.at[
            rows_at(lax.rem(place + line - off, line) * 2 + core, hub_rows)
        ]
        relays.append(
            remote(source, source, relay_send.at[off], relay_recv.at[off], dom, sibling)
        )
        relays[-1].start()
    lax.fori_loop(blocks // 2, blocks, local_sum, 0)
    for copy in hub_copies[:1] + relays + dom_copies:
        copy.wait()


def layer_kernel(
    span,
    hub_size,
    weight_rows,
    local_ids,
    halo_ids,
    hub_ids,
    feats_ref,
    local_sum_ref,
    halo_ref,
    hub_ref,
    local_tiles,
    halo_tiles,
    hub_tiles,
    degree_ref,
    out_grad_ref,
    w_self_ref,
    w_neigh_ref,
    bias_ref,
    layer_ref,
    own_ref,
    halo_back_ref,
    payload_ref,
    bias_part_ref,
    halo_acc,
    hub_acc,
    weight_acc,
    bias_acc,
):
    step = pl.program_id(0)
    width = feats_ref.shape[1]

    @pl.when(step == 0)
    def _():
        own_ref[...] = jnp.zeros_like(own_ref)
        halo_acc[...] = jnp.zeros_like(halo_acc)
        hub_acc[...] = jnp.zeros_like(hub_acc)
        weight_acc[...] = jnp.zeros_like(weight_acc)
        bias_acc[...] = jnp.zeros_like(bias_acc)

    groups = (
        (lambda k, block: local_ids[k, 0, block], local_tiles, None, own_ref),
        (lambda k, block: halo_ids[k, block], halo_tiles, halo_ref, halo_acc),
        (lambda k, block: hub_ids[k, block], hub_tiles, hub_ref, hub_acc),
    )
    features = feats_ref[...]
    scales = []
    sums = []
    for sub in range(span):
        block = step * span + sub
        scale = 1.0 / degree_ref[pl.ds(block, 1), :].astype(F32)
        scale = jnp.broadcast_to(scale, (128, 128)).T
        scales.append(jnp.concatenate([scale] * (width // 128), axis=1))
        tiles = []
        sources = []
        for ids, tile_ref, source_ref, _ in groups[1:]:
            for k in range(tile_ref.shape[1]):
                tiles.append(tile_ref[sub, k])
                sources.append(source_ref[rows_at(ids(k, block), 128), :])
        total = local_sum_ref[sub * 128 : (sub + 1) * 128, :] + jnp.dot(
            jnp.concatenate(tiles, axis=1),
            jnp.concatenate(sources, axis=0),
            preferred_element_type=F32,
        )
        sums.append((total * scales[-1]).astype(BF16))
    aggregate = jnp.concatenate(sums, axis=0)
    preact = (
        jnp.dot(features, w_self_ref[...], preferred_element_type=F32)
        + jnp.dot(aggregate, w_neigh_ref[...], preferred_element_type=F32)
        + bias_ref[...]
    )
    sigmoid = 1.0 / (1.0 + jnp.exp(-preact))
    layer_ref[...] = (preact * sigmoid).astype(BF16)
    grad_wide = out_grad_ref[...].astype(F32) * (sigmoid * (1.0 + preact * (1.0 - sigmoid)))
    grad_pre = grad_wide.astype(BF16)
    bias_acc[...] += jnp.sum(
        grad_pre.astype(F32).reshape(span * 16, 8, width), axis=0
    )
    contract_rows = (((0,), (0,)), ((), ()))
    contract_cols = (((1,), (1,)), ((), ()))
    weight_acc[...] += lax.dot_general(
        jnp.concatenate([features, aggregate], axis=1),
        grad_pre,
        contract_rows,
        preferred_element_type=F32,
    )
    own_ref[rows_at(step, span * 128), :] += lax.dot_general(
        grad_pre, w_self_ref[...], contract_cols, preferred_element_type=F32
    )
    back = lax.dot_general(grad_pre, w_neigh_ref[...], contract_cols, preferred_element_type=F32)
    for sub in range(span):
        block = step * span + sub
        scaled = (back[sub * 128 : (sub + 1) * 128, :] * scales[sub]).astype(BF16)
        for ids, tile_ref, _, acc_ref in groups:
            for k in range(tile_ref.shape[1]):
                acc_ref[rows_at(ids(k, block), 128), :] += lax.dot_general(
                    tile_ref[sub, k], scaled, contract_rows, preferred_element_type=F32
                )

    @pl.when(step == pl.num_programs(0) - 1)
    def _():
        halo_back_ref[...] = halo_acc[...].astype(BF16)
        hub_rows = hub_acc.shape[0] // hub_size
        pieces, line, unit = payload_ref.shape[1:4]
        for peer in range(hub_size):
            for piece in range(pieces):
                first = piece * unit
                parts = []
                if first < weight_rows:
                    end = min(first + unit, weight_rows)
                    base = peer * weight_rows
                    parts.append(weight_acc[base + first : base + end, :])
                low = max(first - weight_rows, 0)
                high = min(first + unit - weight_rows, hub_rows)
                if low < high:
                    base = peer * hub_rows
                    parts.append(hub_acc[base + low : base + high, :])
                rest = unit - sum(part.shape[0] for part in parts)
                if rest:
                    parts.append(jnp.zeros((rest, width), F32))
                at = 0
                for part in parts:
                    payload_ref[peer % 2, piece, peer // 2, at : at + part.shape[0], :] = part
                    at += part.shape[0]
        bias_part_ref[...] = bias_acc[...]


def reduce_kernel(
    dom_size,
    hub_size,
    weight_rows,
    halo_back_ref,
    payload_hbm,
    bias_part_ref,
    returned,
    weights,
    gathered,
    bias_out_ref,
    mine,
    core_land,
    line_out,
    line_land,
    held,
    partial,
    dom_land,
    bias_hub,
    bias_dom,
    load_sem,
    core_send,
    core_recv,
    line_send,
    line_recv,
    bias_hub_send,
    bias_hub_recv,
    back_send,
    back_recv,
    dom_send,
    dom_recv,
    bias_dom_send,
    bias_dom_recv,
    gather_send,
    gather_recv,
    weight_send,
    weight_recv,
    relay_send,
    relay_recv,
):
    dom = lax.axis_index("dom")
    hub = lax.axis_index("hub")
    cap = returned.shape[0] // dom_size
    pieces, line, unit, width = mine.shape
    share = unit // dom_size
    core = lax.rem(hub, 2)
    place = hub // 2
    sibling = hub + 1 - 2 * core
    load = pltpu.make_async_copy(payload_hbm.at[core], mine, load_sem)
    load.start()
    barrier = greet(dom_size, hub_size, dom, hub)
    bias_hub[hub] = bias_part_ref[...]
    returned[rows_at(dom, cap), :] = halo_back_ref[rows_at(dom, cap), :]
    pl.semaphore_wait(barrier, hub_size + dom_size - 2)

    core_copies = []
    for q in range(pieces):
        core_copies.append(
            remote(
                payload_hbm.at[1 - core, q],
                core_land.at[q],
                core_send.at[q],
                core_recv.at[q],
                dom,
                sibling,
            )
        )
        core_copies[-1].start()
    bias_copies = []
    for off in range(1, hub_size):
        bias_copies.append(
            remote(
                bias_part_ref,
                bias_hub.at[hub],
                bias_hub_send.at[off],
                bias_hub_recv.at[off],
                dom,
                lax.rem(hub + off, hub_size),
            )
        )
        bias_copies[-1].start()
    back_copies = []
    for off in range(1, dom_size):
        target = lax.rem(dom + off, dom_size)
        back_copies.append(
            remote(
                halo_back_ref.at[rows_at(target, cap)],
                returned.at[rows_at(dom, cap)],
                back_send.at[off],
                back_recv.at[off],
                target,
                hub,
            )
        )
        back_copies[-1].start()
    load.wait()
    line_copies = []
    for q in range(pieces):
        core_copies[q].wait()
        line_copies.append([])
        for off in range(1, line):
            target = lax.rem(place + off, line)
            line_out[q, off] = (mine[q, target] + core_land[q, target]).astype(BF16)
            copy = remote(
                line_out.at[q, off],
                line_land.at[q, off],
                line_send.at[q, off],
                line_recv.at[q, off],
                dom,
                target * 2 + core,
            )
            copy.start()
            line_copies[q].append(copy)
    for copy in bias_copies:
        copy.wait()
    bias_total = bias_hub[0]
    for peer in range(1, hub_size):
        bias_total = bias_total + bias_hub[peer]
    bias_dom[dom] = bias_total
    bias_copies = []
    for off in range(1, dom_size):
        bias_copies.append(
            remote(
                bias_dom.at[dom],
                bias_dom.at[dom],
                bias_dom_send.at[off],
                bias_dom_recv.at[off],
                lax.rem(dom + off, dom_size),
                hub,
            )
        )
        bias_copies[-1].start()
    dom_copies = []
    for q in range(pieces):
        total = mine[q, place] + core_land[q, place]
        for copy in line_copies[q]:
            copy.wait()
        for off in range(1, line):
            total = total + line_land[q, off].astype(F32)
        held[q] = total
        partial[q] = total.astype(BF16)
        dom_copies.append([])
        for off in range(1, dom_size):
            target = lax.rem(dom + off, dom_size)
            copy = remote(
                partial.at[q, rows_at(target, share)],
                dom_land.at[q, off],
                dom_send.at[q, off],
                dom_recv.at[q, off],
                target,
                hub,
            )
            copy.start()
            dom_copies[q].append(copy)
    gather_copies = []
    for q in range(pieces):
        for copy in dom_copies[q]:
            copy.wait()
        total = held[q, rows_at(dom, share), :]
        for off in range(1, dom_size):
            total = total + dom_land[q, off].astype(F32)
        gathered[q, rows_at(dom, share), :] = total.astype(BF16)
        gather_copies.append([])
        for off in range(1, dom_size):
            copy = remote(
                gathered.at[q, rows_at(dom, share)],
                gathered.at[q, rows_at(dom, share)],
                gather_send.at[q, off],
                gather_recv.at[q, off],
                lax.rem(dom + off, dom_size),
                hub,
            )
            copy.start()
            gather_copies[q].append(copy)

    for copy in gather_copies[0]:
        copy.wait()
    weights[hub] = gathered[0, :weight_rows, :]
    weight_copies = []
    for off in range(line):
        weight_copies.append(
            remote(
                gathered.at[0, pl.ds(0, weight_rows)],
                weights.at[hub],
                weight_send.at[off],
                weight_recv.at[off],
                dom,
                sibling if off == 0 else lax.rem(place + off, line) * 2 + core,
            )
        )
    for copy in weight_copies[1:] + weight_copies[:1]:
        copy.start()

    for copy in back_copies + bias_copies:
        copy.wait()
    bias_total = bias_dom[0]
    for peer in range(1, dom_size):
        bias_total = bias_total + bias_dom[peer]
    bias_out_ref[...] = bias_total
    relays = []
    for off in range(1, line):
        weight_copies[off].wait()
        source = weights.at[lax.rem(place + line - off, line) * 2 + core]
        relays.append(
            remote(source, source, relay_send.at[off], relay_recv.at[off], dom, sibling)
        )
        relays[-1].start()
    for copies in gather_copies[1:]:
        for copy in copies:
            copy.wait()
    for copy in weight_copies[:1] + relays:
        copy.wait()


def finish_kernel(
    weight_rows,
    factor,
    column_ref,
    own_ref,
    returned_ref,
    weights_ref,
    gathered_ref,
    bias_ref,
    feats_grad_ref,
    self_ref,
    neigh_ref,
    bias_out_ref,
    hub_out_ref,
):
    step = pl.program_id(0)
    rows, width = own_ref.shape
    slots = returned_ref.shape[0]

    @pl.when(step == 0)
    def _():
        pieces, unit = gathered_ref.shape[:2]
        hub_rows = hub_out_ref.shape[0]
        for q in range(pieces):
            low = max(q * unit, weight_rows)
            high = min((q + 1) * unit, weight_rows + hub_rows)
            if low < high:
                hub_out_ref[low - weight_rows : high - weight_rows, :] = gathered_ref[
                    q, low - q * unit : high - q * unit, :
                ].astype(F32)
        half = weights_ref.shape[0] // 2
        self_ref[...] = weights_ref[:half].reshape(width, width).astype(F32) * factor
        neigh_ref[...] = weights_ref[half:].reshape(width, width).astype(F32) * factor
        bias_out_ref[...] = jnp.sum(bias_ref[...], axis=0, keepdims=True) * factor

    row = lax.broadcasted_iota(jnp.int32, (rows, slots), 0) + step * rows
    onehot = (row.astype(F32) == column_ref[0:1, :]).astype(F32).astype(BF16)
    feats_grad_ref[...] = (
        own_ref[...] + jnp.dot(onehot, returned_ref[...], preferred_element_type=F32)
    ).astype(BF16)


def body(
    node_feats,
    hub_feats,
    w_self,
    w_neigh,
    out_bias,
    send_rows,
    send_counts,
    local_ids,
    local_tiles,
    halo_ids,
    halo_tiles,
    hub_ids,
    hub_tiles,
    degree,
    out_grad,
):
    dom_size = lax.axis_size("dom")
    hub_size = lax.axis_size("hub")
    rows, width = node_feats.shape[2:]
    tile = local_tiles.shape[-1]
    blocks = rows // tile
    cap = send_rows.shape[-1]
    slots = dom_size * cap
    hub_rows = hub_feats.shape[0]
    features = node_feats.reshape(rows, width)
    dma = pltpu.SemaphoreType.DMA
    any_spec = pl.BlockSpec(memory_space=pl.ANY)
    counts = (local_tiles.shape[3], halo_tiles.shape[3], hub_tiles.shape[3])
    local_sets = local_tiles.reshape(blocks, counts[0], tile, tile)
    local_table = jnp.transpose(local_ids, (0, 3, 1, 2)).reshape(counts[0], 1, blocks)
    halo_table = jnp.transpose(halo_ids, (0, 1, 3, 2)).reshape(counts[1], blocks)
    hub_table = jnp.transpose(hub_ids, (0, 1, 3, 2)).reshape(counts[2], blocks)
    line = hub_size // 2

    halo, hub_all, column, local_sum = pl.pallas_call(
        functools.partial(exchange_kernel, dom_size, hub_size),
        out_shape=(
            jax.ShapeDtypeStruct((slots, width), BF16),
            jax.ShapeDtypeStruct((hub_size * hub_rows, width), BF16),
            jax.ShapeDtypeStruct((8, slots), F32),
            jax.ShapeDtypeStruct((rows, width), F32),
        ),
        in_specs=[pl.BlockSpec(memory_space=pltpu.SMEM)] + [any_spec] * 5,
        out_specs=(VMEM_SPEC,) * 4,
        scratch_shapes=[
            pltpu.VMEM((dom_size, cap), jnp.int32),
            pltpu.VMEM((1, dom_size), jnp.int32),
            pltpu.VMEM((blocks, tile, width), BF16),
            pltpu.VMEM((blocks, counts[0], tile, tile), BF16),
            pltpu.VMEM((128, 128), F32),
            pltpu.VMEM((slots, width), BF16),
            dma((5,)),
            dma((line,)),
            dma((line,)),
            dma((line,)),
            dma((line,)),
            dma((dom_size,)),
            dma((dom_size,)),
        ],
        compiler_params=pltpu.CompilerParams(
            collective_id=0, has_side_effects=True, vmem_limit_bytes=VMEM_LIMIT
        ),
        name="exchange",
    )(
        local_table,
        send_rows.reshape(dom_size, cap),
        send_counts.reshape(1, dom_size),
        node_feats.reshape(blocks, tile, width),
        hub_feats,
        local_sets,
    )

    span = 4
    weight_rows = 2 * width // hub_size
    unit = 16 * dom_size
    pieces = (weight_rows + hub_rows + unit - 1) // unit
    whole = lambda *shape: pl.BlockSpec(shape, lambda i, *_: (0,) * len(shape))
    tiles = lambda count: pl.BlockSpec((span, count, tile, tile), lambda i, *_: (i, 0, 0, 0))
    moving = pl.BlockSpec((span * tile, width), lambda i, *_: (i, 0))
    layer_rows, own_grad, halo_back, payload, bias_part = pl.pallas_call(
        functools.partial(layer_kernel, span, hub_size, weight_rows),
        out_shape=(
            jax.ShapeDtypeStruct((rows, width), BF16),
            jax.ShapeDtypeStruct((rows, width), F32),
            jax.ShapeDtypeStruct((slots, width), BF16),
            jax.ShapeDtypeStruct((2, pieces, line, unit, width), F32),
            jax.ShapeDtypeStruct((8, width), F32),
        ),
        grid_spec=pltpu.PrefetchScalarGridSpec(
            num_scalar_prefetch=3,
            grid=(blocks // span,),
            in_specs=[
                moving,
                moving,
                whole(slots, width),
                whole(hub_size * hub_rows, width),
                tiles(counts[0]),
                tiles(counts[1]),
                tiles(counts[2]),
                whole(blocks, tile),
                moving,
                whole(width, width),
                whole(width, width),
                whole(1, width),
            ],
            out_specs=(
                moving,
                whole(rows, width),
                whole(slots, width),
                whole(2, pieces, line, unit, width),
                whole(8, width),
            ),
            scratch_shapes=[
                pltpu.VMEM((slots, width), F32),
                pltpu.VMEM((hub_size * hub_rows, width), F32),
                pltpu.VMEM((2 * width, width), F32),
                pltpu.VMEM((8, width), F32),
            ],
        ),
        compiler_params=pltpu.CompilerParams(vmem_limit_bytes=VMEM_LIMIT),
        name="layer",
    )(
        local_table,
        halo_table,
        hub_table,
        features,
        local_sum,
        halo,
        hub_all,
        local_sets,
        halo_tiles.reshape(blocks, counts[1], tile, tile),
        hub_tiles.reshape(blocks, counts[2], tile, tile),
        degree.reshape(blocks, tile),
        out_grad.reshape(rows, width),
        w_self,
        w_neigh,
        out_bias.reshape(1, width),
    )

    factor = 1.0 / math.sqrt(rows * dom_size * hub_size)
    share = unit // dom_size
    pairs = [dma((pieces,))] * 2 + [dma((pieces, line))] * 2 + [dma((hub_size,))] * 2
    pairs += [dma((dom_size,))] * 2 + [dma((pieces, dom_size))] * 2 + [dma((dom_size,))] * 2
    pairs += [dma((pieces, dom_size))] * 2 + [dma((line,))] * 4
    returned, weights, gathered, bias_sum = pl.pallas_call(
        functools.partial(reduce_kernel, dom_size, hub_size, weight_rows),
        out_shape=(
            jax.ShapeDtypeStruct((slots, width), BF16),
            jax.ShapeDtypeStruct((hub_size, weight_rows, width), BF16),
            jax.ShapeDtypeStruct((pieces, unit, width), BF16),
            jax.ShapeDtypeStruct((8, width), F32),
        ),
        in_specs=[VMEM_SPEC, any_spec, VMEM_SPEC],
        out_specs=(VMEM_SPEC,) * 4,
        scratch_shapes=[
            pltpu.VMEM((pieces, line, unit, width), F32),
            pltpu.VMEM((pieces, line, unit, width), F32),
            pltpu.VMEM((pieces, line, unit, width), BF16),
            pltpu.VMEM((pieces, line, unit, width), BF16),
            pltpu.VMEM((pieces, unit, width), F32),
            pltpu.VMEM((pieces, unit, width), BF16),
            pltpu.VMEM((pieces, dom_size, share, width), BF16),
            pltpu.VMEM((hub_size, 8, width), F32),
            pltpu.VMEM((dom_size, 8, width), F32),
            dma(()),
        ]
        + pairs,
        compiler_params=pltpu.CompilerParams(
            collective_id=1, has_side_effects=True, vmem_limit_bytes=VMEM_LIMIT
        ),
        name="reduce",
    )(halo_back, payload, bias_part)

    large = pl.BlockSpec((rows // 4, width), lambda i: (i, 0))
    fixed = lambda *shape: pl.BlockSpec(shape, lambda i: (0,) * len(shape))
    feats_grad, grad_self, grad_neigh, grad_bias, hub_grads = pl.pallas_call(
        functools.partial(finish_kernel, weight_rows, factor),
        grid=(4,),
        out_shape=(
            jax.ShapeDtypeStruct((rows, width), BF16),
            jax.ShapeDtypeStruct((width, width), F32),
            jax.ShapeDtypeStruct((width, width), F32),
            jax.ShapeDtypeStruct((1, width), F32),
            jax.ShapeDtypeStruct((hub_rows, width), F32),
        ),
        in_specs=[
            fixed(8, slots),
            large,
            fixed(slots, width),
            fixed(hub_size, weight_rows, width),
            fixed(pieces, unit, width),
            fixed(8, width),
        ],
        out_specs=(
            large,
            fixed(width, width),
            fixed(width, width),
            fixed(1, width),
            fixed(hub_rows, width),
        ),
        compiler_params=pltpu.CompilerParams(vmem_limit_bytes=VMEM_LIMIT),
        name="finish",
    )(column, own_grad, returned, weights, gathered, bias_sum)
    return (
        layer_rows.reshape(node_feats.shape),
        feats_grad.reshape(node_feats.shape),
        grad_self,
        grad_neigh,
        grad_bias.reshape(width),
        hub_grads,
    )


def solution(mesh):
    placed = (
        P("dom", "hub", None, None),
        P("hub", None),
        P(),
        P(),
        P(),
        P("dom", "hub", None, None),
        P("dom", "hub", None),
        P("dom", "hub", None, None),
        P("dom", "hub", None, None, None, None),
        P("dom", "hub", None, None),
        P("dom", "hub", None, None, None, None),
        P("dom", "hub", None, None),
        P("dom", "hub", None, None, None, None),
        P("dom", "hub", None),
        P("dom", "hub", None, None),
    )
    return jax.shard_map(
        body,
        mesh=mesh,
        in_specs=placed,
        out_specs=(
            P("dom", "hub", None, None),
            P("dom", "hub", None, None),
            P(),
            P(),
            P(),
            P("hub", None),
        ),
        check_vma=False,
    )
```

```python
import functools
import math

import jax
import jax.numpy as jnp
from jax import lax
from jax.experimental import pallas as pl
from jax.experimental.pallas import tpu as pltpu
from jax.sharding import PartitionSpec as P

F32 = jnp.float32
BF16 = jnp.bfloat16
MESH = pl.DeviceIdType.MESH
VMEM_SPEC = pl.BlockSpec(memory_space=pltpu.VMEM)
VMEM_LIMIT = 60 * 1024 * 1024


def rows_at(index, size):
    return pl.ds(pl.multiple_of(index * size, size), size)


def greet(dom_size, hub_size, dom, hub):
    barrier = pltpu.get_barrier_semaphore()
    for off in range(1, hub_size):
        pl.semaphore_signal(
            barrier, inc=1, device_id=(dom, lax.rem(hub + off, hub_size)), device_id_type=MESH
        )
    for off in range(1, dom_size):
        pl.semaphore_signal(
            barrier, inc=1, device_id=(lax.rem(dom + off, dom_size), hub), device_id_type=MESH
        )
    return barrier


def remote(src, dst, send, recv, dom, hub):
    return pltpu.make_async_remote_copy(
        src_ref=src,
        dst_ref=dst,
        send_sem=send,
        recv_sem=recv,
        device_id=(dom, hub),
        device_id_type=MESH,
    )


def exchange_kernel(
    dom_size,
    hub_size,
    local_ids,
    rows_hbm,
    counts_hbm,
    feats_hbm,
    hub_hbm,
    tiles_hbm,
    halo_ref,
    hub_all_ref,
    column_ref,
    local_sum_ref,
    rows_in,
    counts_in,
    feats,
    tiles,
    index,
    outgoing,
    load_sem,
    hub_send,
    hub_recv,
    relay_send,
    relay_recv,
    dom_send,
    dom_recv,
):
    dom = lax.axis_index("dom")
    hub = lax.axis_index("hub")
    blocks, tile, width = feats.shape
    row_count = blocks * tile
    hub_rows = hub_hbm.shape[0]
    cap = rows_in.shape[1]
    line = hub_size // 2
    core = lax.rem(hub, 2)
    place = hub // 2
    sibling = hub + 1 - 2 * core
    loads = [
        pltpu.make_async_copy(source, target, load_sem.at[number])
        for number, (source, target) in enumerate(
            (
                (rows_hbm, rows_in),
                (counts_hbm, counts_in),
                (feats_hbm, feats),
                (hub_hbm, hub_all_ref.at[rows_at(hub, hub_rows)]),
                (tiles_hbm, tiles),
            )
        )
    ]
    for load in loads:
        load.start()
    barrier = greet(dom_size, hub_size, dom, hub)
    pl.semaphore_wait(barrier, hub_size + dom_size - 2)
    own_block = hub_all_ref.at[rows_at(hub, hub_rows)]
    hub_copies = []
    for off in range(line):
        target = sibling if off == 0 else lax.rem(place + off, line) * 2 + core
        hub_copies.append(
            remote(hub_hbm, own_block, hub_send.at[off], hub_recv.at[off], dom, target)
        )
    for copy in hub_copies[1:] + hub_copies[:1]:
        copy.start()
    for load in loads[:3]:
        load.wait()
    shape = (dom_size, dom_size)
    diagonal = lax.broadcasted_iota(jnp.int32, shape, 0) == lax.broadcasted_iota(
        jnp.int32, shape, 1
    )
    wide_counts = jnp.broadcast_to(counts_in[...].astype(F32), shape)
    count = jnp.sum(jnp.where(diagonal, wide_counts, 0.0), axis=1, keepdims=True)
    live = lax.broadcasted_iota(jnp.int32, (dom_size, cap), 1).astype(F32) < count
    index[...] = jnp.full((128, 128), -1.0, F32)
    index[:dom_size, :cap] = jnp.where(live, rows_in[...].astype(F32), -1.0)
    turned = index[...].T
    column = jnp.concatenate(
        [
            jnp.broadcast_to(turned[:cap, peer : peer + 1], (cap, 128))
            for peer in range(dom_size)
        ],
        axis=0,
    )
    column_ref[...] = column.T[:8, :]
    lane = lax.broadcasted_iota(jnp.int32, column.shape, 1).astype(F32)
    onehot = jnp.concatenate(
        [
            (column == lane + float(start)).astype(F32).astype(BF16)
            for start in range(0, row_count, 128)
        ],
        axis=1,
    )
    outgoing[...] = jnp.dot(
        onehot, feats[...].reshape(row_count, width), preferred_element_type=F32).astype(BF16)
    dom_copies = []
    for off in range(1, dom_size):
        target = lax.rem(dom + off, dom_size)
        dom_copies.append(
            remote(
                outgoing.at[rows_at(target, cap)],
                halo_ref.at[rows_at(dom, cap)],
                dom_send.at[off],
                dom_recv.at[off],
                target,
                hub,
            )
        )
        dom_copies[-1].start()
    halo_ref[rows_at(dom, cap), :] = outgoing[rows_at(dom, cap), :]
    for load in loads[3:]:
        load.wait()

    def local_sum(group, carry):
        for sub in range(4):
            block = group * 4 + sub
            taken = [tiles[block, k] for k in range(tiles.shape[1])]
            sources = [feats[local_ids[k, 0, block]] for k in range(tiles.shape[1])]
            local_sum_ref[rows_at(block, 128), :] = jnp.dot(
                jnp.concatenate(taken, axis=1),
                jnp.concatenate(sources, axis=0),
                preferred_element_type=F32,
            )
        return carry

    lax.fori_loop(0, blocks // 8, local_sum, 0)
    relays = []
    for off in range(1, line):
        hub_copies[off].wait()
        source = hub_all_ref.at[
            rows_at(lax.rem(place + line - off, line) * 2 + core, hub_rows)
        ]
        relays.append(
            remote(source, source, relay_send.at[off], relay_recv.at[off], dom, sibling)
        )
        relays[-1].start()
    lax.fori_loop(blocks // 8, blocks // 4, local_sum, 0)
    for copy in hub_copies[:1] + relays + dom_copies:
        copy.wait()


def layer_kernel(
    span,
    hub_size,
    weight_rows,
    local_ids,
    halo_ids,
    hub_ids,
    feats_ref,
    local_sum_ref,
    halo_ref,
    hub_ref,
    local_tiles,
    halo_tiles,
    hub_tiles,
    degree_ref,
    out_grad_ref,
    w_self_ref,
    w_neigh_ref,
    bias_ref,
    layer_ref,
    own_out_ref,
    halo_back_ref,
    payload_ref,
    bias_part_ref,
    own_ref,
    halo_acc,
    hub_acc,
    weight_acc,
    bias_acc,
):
    step = pl.program_id(0)
    width = feats_ref.shape[1]

    @pl.when(step == 0)
    def _():
        own_ref[...] = jnp.zeros_like(own_ref)
        halo_acc[...] = jnp.zeros_like(halo_acc)
        hub_acc[...] = jnp.zeros_like(hub_acc)
        weight_acc[...] = jnp.zeros_like(weight_acc)
        bias_acc[...] = jnp.zeros_like(bias_acc)

    groups = (
        (lambda k, block: local_ids[k, 0, block], local_tiles, None, own_ref),
        (lambda k, block: halo_ids[k, block], halo_tiles, halo_ref, halo_acc),
        (lambda k, block: hub_ids[k, block], hub_tiles, hub_ref, hub_acc),
    )
    features = feats_ref[...]
    scales = []
    sums = []
    for sub in range(span):
        block = step * span + sub
        scale = 1.0 / degree_ref[pl.ds(block, 1), :].astype(F32)
        scale = jnp.broadcast_to(scale, (128, 128)).T
        scales.append(jnp.concatenate([scale] * (width // 128), axis=1))
        tiles = []
        sources = []
        for ids, tile_ref, source_ref, _ in groups[1:]:
            for k in range(tile_ref.shape[1]):
                tiles.append(tile_ref[sub, k])
                sources.append(source_ref[rows_at(ids(k, block), 128), :])
        total = local_sum_ref[sub * 128 : (sub + 1) * 128, :] + jnp.dot(
            jnp.concatenate(tiles, axis=1),
            jnp.concatenate(sources, axis=0),
            preferred_element_type=F32,
        )
        sums.append((total * scales[-1]).astype(BF16))
    aggregate = jnp.concatenate(sums, axis=0)
    preact = (
        jnp.dot(features, w_self_ref[...], preferred_element_type=F32)
        + jnp.dot(aggregate, w_neigh_ref[...], preferred_element_type=F32)
        + bias_ref[...]
    )
    sigmoid = 1.0 / (1.0 + jnp.exp(-preact))
    layer_ref[...] = (preact * sigmoid).astype(BF16)
    grad_wide = out_grad_ref[...].astype(F32) * (sigmoid * (1.0 + preact * (1.0 - sigmoid)))
    grad_pre = grad_wide.astype(BF16)
    bias_acc[...] += jnp.sum(
        grad_pre.astype(F32).reshape(span * 16, 8, width), axis=0
    )
    contract_rows = (((0,), (0,)), ((), ()))
    contract_cols = (((1,), (1,)), ((), ()))
    weight_acc[...] += lax.dot_general(
        jnp.concatenate([features, aggregate], axis=1),
        grad_pre,
        contract_rows,
        preferred_element_type=F32,
    )
    own_ref[rows_at(step, span * 128), :] += lax.dot_general(
        grad_pre, w_self_ref[...], contract_cols, preferred_element_type=F32
    )
    back = lax.dot_general(grad_pre, w_neigh_ref[...], contract_cols, preferred_element_type=F32)
    for sub in range(span):
        block = step * span + sub
        scaled = (back[sub * 128 : (sub + 1) * 128, :] * scales[sub]).astype(BF16)
        for ids, tile_ref, _, acc_ref in groups:
            for k in range(tile_ref.shape[1]):
                acc_ref[rows_at(ids(k, block), 128), :] += lax.dot_general(
                    tile_ref[sub, k], scaled, contract_rows, preferred_element_type=F32
                )

    @pl.when(step == pl.num_programs(0) - 1)
    def _():
        own_out_ref[...] = own_ref[...].astype(BF16)
        halo_back_ref[...] = halo_acc[...].astype(BF16)
        hub_rows = hub_acc.shape[0] // hub_size
        pieces, line, unit = payload_ref.shape[1:4]
        for peer in range(hub_size):
            for piece in range(pieces):
                first = piece * unit
                parts = []
                if first < weight_rows:
                    end = min(first + unit, weight_rows)
                    base = peer * weight_rows
                    parts.append(weight_acc[base + first : base + end, :])
                low = max(first - weight_rows, 0)
                high = min(first + unit - weight_rows, hub_rows)
                if low < high:
                    base = peer * hub_rows
                    parts.append(hub_acc[base + low : base + high, :])
                rest = unit - sum(part.shape[0] for part in parts)
                if rest:
                    parts.append(jnp.zeros((rest, width), F32))
                at = 0
                for part in parts:
                    payload_ref[peer % 2, piece, peer // 2, at : at + part.shape[0], :] = part.astype(BF16)
                    at += part.shape[0]
        bias_part_ref[...] = bias_acc[...]


def reduce_kernel(
    dom_size,
    hub_size,
    weight_rows,
    halo_back_ref,
    payload_hbm,
    bias_part_ref,
    returned,
    weights,
    gathered,
    bias_out_ref,
    mine,
    core_land,
    line_out,
    line_land,
    held,
    partial,
    dom_land,
    bias_hub,
    bias_dom,
    load_sem,
    core_send,
    core_recv,
    line_send,
    line_recv,
    bias_hub_send,
    bias_hub_recv,
    back_send,
    back_recv,
    dom_send,
    dom_recv,
    bias_dom_send,
    bias_dom_recv,
    gather_send,
    gather_recv,
    weight_send,
    weight_recv,
    relay_send,
    relay_recv,
):
    dom = lax.axis_index("dom")
    hub = lax.axis_index("hub")
    cap = returned.shape[0] // dom_size
    pieces, line, unit, width = mine.shape
    share = unit // dom_size
    core = lax.rem(hub, 2)
    place = hub // 2
    sibling = hub + 1 - 2 * core
    load = pltpu.make_async_copy(payload_hbm.at[core], mine, load_sem)
    load.start()
    barrier = greet(dom_size, hub_size, dom, hub)
    bias_hub[hub] = bias_part_ref[...]
    returned[rows_at(dom, cap), :] = halo_back_ref[rows_at(dom, cap), :]
    pl.semaphore_wait(barrier, hub_size + dom_size - 2)

    core_copies = []
    for q in range(pieces):
        core_copies.append(
            remote(
                payload_hbm.at[1 - core, q],
                core_land.at[q],
                core_send.at[q],
                core_recv.at[q],
                dom,
                sibling,
            )
        )
        core_copies[-1].start()
    bias_copies = []
    for off in range(1, hub_size):
        bias_copies.append(
            remote(
                bias_part_ref,
                bias_hub.at[hub],
                bias_hub_send.at[off],
                bias_hub_recv.at[off],
                dom,
                lax.rem(hub + off, hub_size),
            )
        )
        bias_copies[-1].start()
    back_copies = []
    for off in range(1, dom_size):
        target = lax.rem(dom + off, dom_size)
        back_copies.append(
            remote(
                halo_back_ref.at[rows_at(target, cap)],
                returned.at[rows_at(dom, cap)],
                back_send.at[off],
                back_recv.at[off],
                target,
                hub,
            )
        )
        back_copies[-1].start()
    load.wait()
    line_copies = []
    for q in range(pieces):
        core_copies[q].wait()
        line_copies.append([])
        for off in range(1, line):
            target = lax.rem(place + off, line)
            line_out[q, off] = (
                mine[q, target].astype(F32) + core_land[q, target].astype(F32)
            ).astype(BF16)
            copy = remote(
                line_out.at[q, off],
                line_land.at[q, off],
                line_send.at[q, off],
                line_recv.at[q, off],
                dom,
                target * 2 + core,
            )
            copy.start()
            line_copies[q].append(copy)
    for copy in bias_copies:
        copy.wait()
    bias_total = bias_hub[0]
    for peer in range(1, hub_size):
        bias_total = bias_total + bias_hub[peer]
    bias_dom[dom] = bias_total
    bias_copies = []
    for off in range(1, dom_size):
        bias_copies.append(
            remote(
                bias_dom.at[dom],
                bias_dom.at[dom],
                bias_dom_send.at[off],
                bias_dom_recv.at[off],
                lax.rem(dom + off, dom_size),
                hub,
            )
        )
        bias_copies[-1].start()
    dom_copies = []
    for q in range(pieces):
        total = mine[q, place].astype(F32) + core_land[q, place].astype(F32)
        for copy in line_copies[q]:
            copy.wait()
        for off in range(1, line):
            total = total + line_land[q, off].astype(F32)
        held[q] = total
        partial[q] = total.astype(BF16)
        dom_copies.append([])
        for off in range(1, dom_size):
            target = lax.rem(dom + off, dom_size)
            copy = remote(
                partial.at[q, rows_at(target, share)],
                dom_land.at[q, off],
                dom_send.at[q, off],
                dom_recv.at[q, off],
                target,
                hub,
            )
            copy.start()
            dom_copies[q].append(copy)
    gather_copies = []
    for q in range(pieces):
        for copy in dom_copies[q]:
            copy.wait()
        total = held[q, rows_at(dom, share), :]
        for off in range(1, dom_size):
            total = total + dom_land[q, off].astype(F32)
        gathered[q, rows_at(dom, share), :] = total.astype(BF16)
        gather_copies.append([])
        for off in range(1, dom_size):
            copy = remote(
                gathered.at[q, rows_at(dom, share)],
                gathered.at[q, rows_at(dom, share)],
                gather_send.at[q, off],
                gather_recv.at[q, off],
                lax.rem(dom + off, dom_size),
                hub,
            )
            copy.start()
            gather_copies[q].append(copy)

    for copy in gather_copies[0]:
        copy.wait()
    weights[hub] = gathered[0, :weight_rows, :]
    weight_copies = []
    for off in range(line):
        weight_copies.append(
            remote(
                gathered.at[0, pl.ds(0, weight_rows)],
                weights.at[hub],
                weight_send.at[off],
                weight_recv.at[off],
                dom,
                sibling if off == 0 else lax.rem(place + off, line) * 2 + core,
            )
        )
    for copy in weight_copies[1:] + weight_copies[:1]:
        copy.start()

    for copy in back_copies + bias_copies:
        copy.wait()
    bias_total = bias_dom[0]
    for peer in range(1, dom_size):
        bias_total = bias_total + bias_dom[peer]
    bias_out_ref[...] = bias_total
    relays = []
    for off in range(1, line):
        weight_copies[off].wait()
        source = weights.at[lax.rem(place + line - off, line) * 2 + core]
        relays.append(
            remote(source, source, relay_send.at[off], relay_recv.at[off], dom, sibling)
        )
        relays[-1].start()
    for copies in gather_copies[1:]:
        for copy in copies:
            copy.wait()
    for copy in weight_copies[:1] + relays:
        copy.wait()


def finish_kernel(
    weight_rows,
    factor,
    column_ref,
    own_ref,
    returned_ref,
    weights_ref,
    gathered_ref,
    bias_ref,
    feats_grad_ref,
    self_ref,
    neigh_ref,
    bias_out_ref,
    hub_out_ref,
):
    step = pl.program_id(0)
    rows, width = own_ref.shape
    slots = returned_ref.shape[0]

    @pl.when(step == 0)
    def _():
        pieces, unit = gathered_ref.shape[:2]
        hub_rows = hub_out_ref.shape[0]
        for q in range(pieces):
            low = max(q * unit, weight_rows)
            high = min((q + 1) * unit, weight_rows + hub_rows)
            if low < high:
                hub_out_ref[low - weight_rows : high - weight_rows, :] = gathered_ref[
                    q, low - q * unit : high - q * unit, :
                ].astype(F32)
        half = weights_ref.shape[0] // 2
        self_ref[...] = weights_ref[:half].reshape(width, width).astype(F32) * factor
        neigh_ref[...] = weights_ref[half:].reshape(width, width).astype(F32) * factor
        bias_out_ref[...] = jnp.sum(bias_ref[...], axis=0, keepdims=True) * factor

    row = lax.broadcasted_iota(jnp.int32, (rows, slots), 0) + step * rows
    onehot = (row.astype(F32) == column_ref[0:1, :]).astype(F32).astype(BF16)
    feats_grad_ref[...] = (
        own_ref[...].astype(F32) + jnp.dot(onehot, returned_ref[...], preferred_element_type=F32)
    ).astype(BF16)


def body(
    node_feats,
    hub_feats,
    w_self,
    w_neigh,
    out_bias,
    send_rows,
    send_counts,
    local_ids,
    local_tiles,
    halo_ids,
    halo_tiles,
    hub_ids,
    hub_tiles,
    degree,
    out_grad,
):
    dom_size = lax.axis_size("dom")
    hub_size = lax.axis_size("hub")
    rows, width = node_feats.shape[2:]
    tile = local_tiles.shape[-1]
    blocks = rows // tile
    cap = send_rows.shape[-1]
    slots = dom_size * cap
    hub_rows = hub_feats.shape[0]
    features = node_feats.reshape(rows, width)
    dma = pltpu.SemaphoreType.DMA
    any_spec = pl.BlockSpec(memory_space=pl.ANY)
    counts = (local_tiles.shape[3], halo_tiles.shape[3], hub_tiles.shape[3])
    local_sets = local_tiles.reshape(blocks, counts[0], tile, tile)
    local_table = jnp.transpose(local_ids, (0, 3, 1, 2)).reshape(counts[0], 1, blocks)
    halo_table = jnp.transpose(halo_ids, (0, 1, 3, 2)).reshape(counts[1], blocks)
    hub_table = jnp.transpose(hub_ids, (0, 1, 3, 2)).reshape(counts[2], blocks)
    line = hub_size // 2

    halo, hub_all, column, local_sum = pl.pallas_call(
        functools.partial(exchange_kernel, dom_size, hub_size),
        out_shape=(
            jax.ShapeDtypeStruct((slots, width), BF16),
            jax.ShapeDtypeStruct((hub_size * hub_rows, width), BF16),
            jax.ShapeDtypeStruct((8, slots), F32),
            jax.ShapeDtypeStruct((rows, width), F32),
        ),
        in_specs=[pl.BlockSpec(memory_space=pltpu.SMEM)] + [any_spec] * 5,
        out_specs=(VMEM_SPEC,) * 4,
        scratch_shapes=[
            pltpu.VMEM((dom_size, cap), jnp.int32),
            pltpu.VMEM((1, dom_size), jnp.int32),
            pltpu.VMEM((blocks, tile, width), BF16),
            pltpu.VMEM((blocks, counts[0], tile, tile), BF16),
            pltpu.VMEM((128, 128), F32),
            pltpu.VMEM((slots, width), BF16),
            dma((5,)),
            dma((line,)),
            dma((line,)),
            dma((line,)),
            dma((line,)),
            dma((dom_size,)),
            dma((dom_size,)),
        ],
        compiler_params=pltpu.CompilerParams(
            collective_id=0, has_side_effects=True, vmem_limit_bytes=VMEM_LIMIT
        ),
        name="exchange",
    )(
        local_table,
        send_rows.reshape(dom_size, cap),
        send_counts.reshape(1, dom_size),
        node_feats.reshape(blocks, tile, width),
        hub_feats,
        local_sets,
    )

    span = 4
    weight_rows = 2 * width // hub_size
    unit = 16 * dom_size
    pieces = (weight_rows + hub_rows + unit - 1) // unit
    whole = lambda *shape: pl.BlockSpec(shape, lambda i, *_: (0,) * len(shape))
    tiles = lambda count: pl.BlockSpec((span, count, tile, tile), lambda i, *_: (i, 0, 0, 0))
    moving = pl.BlockSpec((span * tile, width), lambda i, *_: (i, 0))
    layer_rows, own_grad, halo_back, payload, bias_part = pl.pallas_call(
        functools.partial(layer_kernel, span, hub_size, weight_rows),
        out_shape=(
            jax.ShapeDtypeStruct((rows, width), BF16),
            jax.ShapeDtypeStruct((rows, width), BF16),
            jax.ShapeDtypeStruct((slots, width), BF16),
            jax.ShapeDtypeStruct((2, pieces, line, unit, width), BF16),
            jax.ShapeDtypeStruct((8, width), F32),
        ),
        grid_spec=pltpu.PrefetchScalarGridSpec(
            num_scalar_prefetch=3,
            grid=(blocks // span,),
            in_specs=[
                moving,
                moving,
                whole(slots, width),
                whole(hub_size * hub_rows, width),
                tiles(counts[0]),
                tiles(counts[1]),
                tiles(counts[2]),
                whole(blocks, tile),
                moving,
                whole(width, width),
                whole(width, width),
                whole(1, width),
            ],
            out_specs=(
                moving,
                whole(rows, width),
                whole(slots, width),
                whole(2, pieces, line, unit, width),
                whole(8, width),
            ),
            scratch_shapes=[
                pltpu.VMEM((rows, width), F32),
                pltpu.VMEM((slots, width), F32),
                pltpu.VMEM((hub_size * hub_rows, width), F32),
                pltpu.VMEM((2 * width, width), F32),
                pltpu.VMEM((8, width), F32),
            ],
        ),
        compiler_params=pltpu.CompilerParams(vmem_limit_bytes=VMEM_LIMIT),
        name="layer",
    )(
        local_table,
        halo_table,
        hub_table,
        features,
        local_sum,
        halo,
        hub_all,
        local_sets,
        halo_tiles.reshape(blocks, counts[1], tile, tile),
        hub_tiles.reshape(blocks, counts[2], tile, tile),
        degree.reshape(blocks, tile),
        out_grad.reshape(rows, width),
        w_self,
        w_neigh,
        out_bias.reshape(1, width),
    )

    factor = 1.0 / math.sqrt(rows * dom_size * hub_size)
    share = unit // dom_size
    pairs = [dma((pieces,))] * 2 + [dma((pieces, line))] * 2 + [dma((hub_size,))] * 2
    pairs += [dma((dom_size,))] * 2 + [dma((pieces, dom_size))] * 2 + [dma((dom_size,))] * 2
    pairs += [dma((pieces, dom_size))] * 2 + [dma((line,))] * 4
    returned, weights, gathered, bias_sum = pl.pallas_call(
        functools.partial(reduce_kernel, dom_size, hub_size, weight_rows),
        out_shape=(
            jax.ShapeDtypeStruct((slots, width), BF16),
            jax.ShapeDtypeStruct((hub_size, weight_rows, width), BF16),
            jax.ShapeDtypeStruct((pieces, unit, width), BF16),
            jax.ShapeDtypeStruct((8, width), F32),
        ),
        in_specs=[VMEM_SPEC, any_spec, VMEM_SPEC],
        out_specs=(VMEM_SPEC,) * 4,
        scratch_shapes=[
            pltpu.VMEM((pieces, line, unit, width), BF16),
            pltpu.VMEM((pieces, line, unit, width), BF16),
            pltpu.VMEM((pieces, line, unit, width), BF16),
            pltpu.VMEM((pieces, line, unit, width), BF16),
            pltpu.VMEM((pieces, unit, width), F32),
            pltpu.VMEM((pieces, unit, width), BF16),
            pltpu.VMEM((pieces, dom_size, share, width), BF16),
            pltpu.VMEM((hub_size, 8, width), F32),
            pltpu.VMEM((dom_size, 8, width), F32),
            dma(()),
        ]
        + pairs,
        compiler_params=pltpu.CompilerParams(
            collective_id=1, has_side_effects=True, vmem_limit_bytes=VMEM_LIMIT
        ),
        name="reduce",
    )(halo_back, payload, bias_part)

    large = pl.BlockSpec((rows // 4, width), lambda i: (i, 0))
    fixed = lambda *shape: pl.BlockSpec(shape, lambda i: (0,) * len(shape))
    feats_grad, grad_self, grad_neigh, grad_bias, hub_grads = pl.pallas_call(
        functools.partial(finish_kernel, weight_rows, factor),
        grid=(4,),
        out_shape=(
            jax.ShapeDtypeStruct((rows, width), BF16),
            jax.ShapeDtypeStruct((width, width), F32),
            jax.ShapeDtypeStruct((width, width), F32),
            jax.ShapeDtypeStruct((1, width), F32),
            jax.ShapeDtypeStruct((hub_rows, width), F32),
        ),
        in_specs=[
            fixed(8, slots),
            large,
            fixed(slots, width),
            fixed(hub_size, weight_rows, width),
            fixed(pieces, unit, width),
            fixed(8, width),
        ],
        out_specs=(
            large,
            fixed(width, width),
            fixed(width, width),
            fixed(1, width),
            fixed(hub_rows, width),
        ),
        compiler_params=pltpu.CompilerParams(vmem_limit_bytes=VMEM_LIMIT),
        name="finish",
    )(column, own_grad, returned, weights, gathered, bias_sum)
    return (
        layer_rows.reshape(node_feats.shape),
        feats_grad.reshape(node_feats.shape),
        grad_self,
        grad_neigh,
        grad_bias.reshape(width),
        hub_grads,
    )


def solution(mesh):
    placed = (
        P("dom", "hub", None, None),
        P("hub", None),
        P(),
        P(),
        P(),
        P("dom", "hub", None, None),
        P("dom", "hub", None),
        P("dom", "hub", None, None),
        P("dom", "hub", None, None, None, None),
        P("dom", "hub", None, None),
        P("dom", "hub", None, None, None, None),
        P("dom", "hub", None, None),
        P("dom", "hub", None, None, None, None),
        P("dom", "hub", None),
        P("dom", "hub", None, None),
    )
    return jax.shard_map(
        body,
        mesh=mesh,
        in_specs=placed,
        out_specs=(
            P("dom", "hub", None, None),
            P("dom", "hub", None, None),
            P(),
            P(),
            P(),
            P("hub", None),
        ),
        check_vma=False,
    )
```
